128 devices in a mesh: rep: 2 (over x_hi), fsdp: 16 (over y, x_lo, core), tp: 4 (over z).
Axes of the slice: x: 4 (x_hi: 2, x_lo: 2; x = x_hi * 2 + x_lo), y: 4, z: 4, core: 2. Of those that a mesh axis runs over, the one named last changes fastest.
Arguments:
- gate_up_master: float32 [2, 4096, 14336], P(None, 'fsdp', ('rep', 'tp')), may hold values from -0.09375 to 0.09375
- gate_up_moment: float32 [2, 4096, 14336], P(None, 'fsdp', ('rep', 'tp')), may hold values from -0.00018310547 to 0.00018310547
- gate_up_second: float32 [2, 4096, 14336], P(None, 'fsdp', ('rep', 'tp')), may hold values from 8.5149493e-10 to 8.51495e-09
- gate_up_grad: bfloat16 [2, 4096, 14336], P(None, 'fsdp', ('rep', 'tp')), may hold values from -8 to 8
- down_master: float32 [4096, 14336], P('fsdp', ('rep', 'tp')), may hold values from -0.046875 to 0.046875
- down_moment: float32 [4096, 14336], P('fsdp', ('rep', 'tp')), may hold values from -0.00018310547 to 0.00018310547
- down_second: float32 [4096, 14336], P('fsdp', ('rep', 'tp')), may hold values from 8.5149493e-10 to 8.51495e-09
- down_grad: bfloat16 [4096, 14336], P('fsdp', ('rep', 'tp')), may hold values from -8 to 8
- norm_gain: float32 [4096], replicated, may hold values from 0.1 to 1.9
- start_rows: bfloat16 [1024, 4096], P(('rep', 'fsdp', 'tp')), may hold values from -6 to 6
- queries: bfloat16 [2, 1024, 4096], P(None, ('rep', 'fsdp', 'tp')), may hold values from -6 to 6
- new_kv: bfloat16 [2, 1024, 2, 1024], P(None, ('rep', 'fsdp', 'tp')), may hold values from -6 to 6
- kv_pool: bfloat16 [8192, 16, 2, 1024], P(('rep', 'fsdp', 'tp')), may hold values from -6 to 6
- page_table: int32 [1024, 8], P(('rep', 'fsdp', 'tp')), may hold values from 0 to 63, as said below
- cache_len: int32 [1024], P(('rep', 'fsdp', 'tp')), may hold values from 1 to 128, as said below
Outputs:
- final_rows: bfloat16 [1024, 4096], P(('rep', 'fsdp', 'tp'))
The draws below stay inside these ranges and needn't reach their ends.
Inputs may be any that keep to these rules, and one draw needn't show every extreme that they name: `page_table`: within each aligned block of 8 rows, the entries name each of the 64 pages of that block exactly once. `cache_len`: some row has exactly 128 cached positions.
All inputs are finite; a program needn't handle non-finite values.
Results may differ from the reference program's by a relative error of at most 0.019.
Values may be sent and summed in bfloat16 or wider, within the bound.
No kernel may reach another device: no remote copies, remote signals or barrier semaphores. Data moves between devices by JAX's collectives and lax.ppermute only.
A program may use at most 128 MiB of HBM per device.

```python
import math
import jax
import jax.numpy as jnp
from jax import lax

D = 4096
FF = 14336
HD = 128
KVH = 8
GROUP = 4
QH = 32
KVD = 1024
RD = 8
PAGE = 16
PPR = 8
CTX = 128
STEPS = 2
ROWS = 1024
POOL_PAGES = 8192


def make_grad(key, stack):
    k_row, k_col, k_base = jax.random.split(key, 3)
    position = jnp.arange(D, dtype=jnp.float32) / (D - 1)
    col_position = jnp.arange(FF, dtype=jnp.float32) / (FF - 1)
    row_scale = (1.0 + 2.0 * position).reshape(1, D, 1) * jnp.exp(jnp.log(10.0) * jax.random.uniform(k_row, (stack, D, 1)))
    col_scale = (1.0 + 2.0 * col_position).reshape(1, 1, FF) * jnp.exp(jnp.log(10.0) * jax.random.uniform(k_col, (stack, 1, FF)))
    base = jax.random.normal(k_base, (stack, D, FF))
    size = 0.0002
    values = jnp.clip(size * row_scale * col_scale * base, -8.0, 8.0)
    return values.astype(jnp.bfloat16)


def draw_gate_up_grad(key, part):
    return make_grad(jax.random.fold_in(key, 11), 2)


def draw_down_grad(key, part):
    return make_grad(jax.random.fold_in(key, 12), 1)[0]


def draw_kv_pool(key, part):
    k_base = jax.random.fold_in(jax.random.fold_in(key, 21), 0)
    shape = (POOL_PAGES, PAGE, 2, KVD)
    base = jax.random.normal(k_base, shape)
    return jnp.clip(base, -6.0, 6.0).astype(jnp.bfloat16)


def draw_queries(key, part):
    k_base = jax.random.fold_in(jax.random.fold_in(key, 22), 0)
    shape = (STEPS, ROWS, QH, HD)
    base = jax.random.normal(k_base, shape)
    return jnp.clip(base, -6.0, 6.0).reshape(STEPS, ROWS, QH * HD).astype(jnp.bfloat16)


def draw_page_table(key, part):
    blocks = ROWS // RD
    keys = jax.random.split(jax.random.fold_in(key, 31), blocks)
    orders = jax.vmap(lambda k: jax.random.permutation(k, RD * PPR))(keys)
    return orders.reshape(ROWS, PPR).astype(jnp.int32)


def draw_cache_len(key, part):
    k_len, k_pick = jax.random.split(jax.random.fold_in(key, 41), 2)
    lengths = jax.random.randint(k_len, (ROWS,), 1, CTX + 1)
    chosen = jax.random.randint(k_pick, (), 0, ROWS)
    return jnp.where(jnp.arange(ROWS) == chosen, CTX, lengths).astype(jnp.int32)


def block_scale(stream_key, shape, cuts, smallest, top_value):
    factor_of, own = 1.0, jax.random.fold_in(stream_key, 6)
    for dim, parts in cuts:
        heights = jnp.exp(jax.random.uniform(jax.random.fold_in(own, dim), (parts,), jnp.float32, smallest / len(cuts), top_value / len(cuts)))
        factor_of = factor_of * jnp.repeat(heights, shape[dim] // parts).reshape([-1 if axis == dim else 1 for axis in range(len(shape))])
    return factor_of


def normal_values(stream_key, dims, scale, most, shards=(), kind=jnp.bfloat16):
    values = scale * jax.random.normal(stream_key, dims, jnp.float32)
    if shards:
        values = values * block_scale(stream_key, dims, shards, -0.22, 0.18)
    return jnp.clip(values, -most, most).astype(kind)


def setup_inputs(seed: int = 0) -> dict:
    key_list = jax.random.split(jax.random.key(seed), 16)
    gate_up_master = normal_values(key_list[0], (2, D, FF), D ** -0.5, 0.09375, ((1, 16), (2, 8)), jnp.float32)
    gate_up_moment = normal_values(key_list[1], (2, D, FF), (0.1 * (D * FF) ** -0.5), 0.00018310547, ((1, 16), (2, 8)), jnp.float32)
    gate_up_second = jnp.clip(jnp.exp(math.log(8.514949634275126e-09) - 2.3025851 * jax.random.uniform(key_list[2], (2, D, FF), jnp.float32) ** block_scale(key_list[2], (2, D, FF), ((1, 16), (2, 8)), -0.2, 0.2)), 8.514949301208219e-10, 8.514949634275126e-09)
    gate_up_grad = draw_gate_up_grad(jax.random.fold_in(key_list[15], 71), 0)
    down_master = normal_values(key_list[4], (D, FF), FF ** -0.5, 0.046875, ((0, 16), (1, 8)), jnp.float32)
    down_moment = normal_values(key_list[5], (D, FF), (0.1 * (D * FF) ** -0.5), 0.00018310547, ((0, 16), (1, 8)), jnp.float32)
    down_second = jnp.clip(jnp.exp(math.log(8.514949634275126e-09) - 2.3025851 * jax.random.uniform(key_list[6], (D, FF), jnp.float32) ** block_scale(key_list[6], (D, FF), ((0, 16), (1, 8)), -0.2, 0.2)), 8.514949301208219e-10, 8.514949634275126e-09)
    down_grad = draw_down_grad(jax.random.fold_in(key_list[15], 71), 0)
    norm_gain = jnp.clip(1.0 + 0.18 * jax.random.normal(key_list[8], (D,), jnp.float32), 0.1, 1.9)
    start_rows = normal_values(key_list[9], (ROWS, D), 1.0, 6.0, ((0, 128),))
    queries = draw_queries(jax.random.fold_in(key_list[15], 71), 0)
    new_kv = normal_values(key_list[11], (STEPS, ROWS, 2, KVD), 1.0, 6.0, ((1, 128),))
    kv_pool = draw_kv_pool(jax.random.fold_in(key_list[15], 71), 0)
    page_table = draw_page_table(jax.random.fold_in(key_list[15], 71), 0)
    cache_len = draw_cache_len(jax.random.fold_in(key_list[15], 71), 0)
    return {"gate_up_master": gate_up_master, "gate_up_moment": gate_up_moment, "gate_up_second": gate_up_second, "gate_up_grad": gate_up_grad, "down_master": down_master, "down_moment": down_moment, "down_second": down_second, "down_grad": down_grad, "norm_gain": norm_gain, "start_rows": start_rows, "queries": queries, "new_kv": new_kv, "kv_pool": kv_pool, "page_table": page_table, "cache_len": cache_len}


beta_one = 0.9
beta_two = 0.95
adam_eps = 1e-08
adam_time = 100.0
norm_eps = 1e-05

def adam_new(master, moment, second, grad, clip):
    learn_rate = 2.0 / D ** 0.5
    g = grad.astype(jnp.float32) * clip
    m = beta_one * moment + (1.0 - beta_one) * g
    v = beta_two * second + (1.0 - beta_two) * g * g
    first_fix = 1.0 - beta_one ** adam_time
    second_fix = 1.0 - beta_two ** adam_time
    return (master - learn_rate * (m / first_fix) / (jnp.sqrt(v / second_fix) + adam_eps)).astype(jnp.bfloat16)

def attend(query, keys, values, valid, fresh_k, fresh_v, step):
    scale = query.shape[-1] ** (-0.5)
    old = jnp.einsum('rjgh,rcjh->rjgc', query.astype(jnp.float32), keys.astype(jnp.float32)) * scale
    old = jnp.where(valid[:, None, None, :], old, -1e+30)
    new = jnp.einsum('rjgh,srjh->rjgs', query.astype(jnp.float32), fresh_k.astype(jnp.float32)) * scale
    allowed = jnp.arange(fresh_k.shape[0]) <= step
    new = jnp.where(allowed[None, None, None, :], new, -1e+30)
    top = jnp.maximum(lax.optimization_barrier(jnp.max(old, axis=-1, keepdims=True)), lax.optimization_barrier(jnp.max(new, axis=-1, keepdims=True)))
    exp_old = jnp.exp(old - top)
    exp_new = jnp.exp(new - top)
    total = lax.optimization_barrier(jnp.sum(exp_old, axis=-1, keepdims=True)) + lax.optimization_barrier(jnp.sum(exp_new, axis=-1, keepdims=True))
    prob_old = (exp_old / total).astype(jnp.bfloat16)
    prob_new = (exp_new / total).astype(jnp.bfloat16)
    out = jnp.einsum('rjgc,rcjh->rjgh', prob_old.astype(jnp.float32), values.astype(jnp.float32))
    out = out + jnp.einsum('rjgs,srjh->rjgh', prob_new.astype(jnp.float32), fresh_v.astype(jnp.float32))
    return out.reshape(out.shape[0], -1)

def reference(gate_up_master, gate_up_moment, gate_up_second, gate_up_grad, down_master, down_moment, down_second, down_grad, norm_gain, start_rows, queries, new_kv, kv_pool, page_table, cache_len):
    total = jnp.sum(jnp.square(gate_up_grad.astype(jnp.float32))) + jnp.sum(jnp.square(down_grad.astype(jnp.float32)))
    clip = jnp.minimum(1.0, 1.0 / jnp.sqrt(total))
    gate_up = adam_new(gate_up_master, gate_up_moment, gate_up_second, gate_up_grad, clip)
    down_t = adam_new(down_master, down_moment, down_second, down_grad, clip)
    owner = (jnp.arange(ROWS, dtype=jnp.int32) // RD).astype(jnp.int32)
    global_page = (owner[:, None] * (RD * PPR) + page_table).astype(jnp.int32)
    cache = kv_pool[global_page].reshape(ROWS, CTX, 2, KVH, HD)
    keys = cache[:, :, 0]
    values = cache[:, :, 1]
    valid = jnp.arange(CTX, dtype=jnp.int32)[None, :] < cache_len[:, None]
    fresh = new_kv.reshape(STEPS, ROWS, 2, KVH, HD)
    fresh_k = fresh[:, :, 0]
    fresh_v = fresh[:, :, 1]
    rows = start_rows
    for step in range(STEPS):
        query = queries[step].reshape(ROWS, KVH, GROUP, HD)
        attended = attend(query, keys, values, valid, fresh_k, fresh_v, step)
        mixed = (rows.astype(jnp.float32) + attended).astype(jnp.bfloat16)
        mixed_f = mixed.astype(jnp.float32)
        normed = (mixed_f * lax.rsqrt(lax.optimization_barrier(jnp.mean(mixed_f * mixed_f, axis=-1, keepdims=True)) + norm_eps) * norm_gain).astype(jnp.bfloat16)
        gate = jnp.dot(normed, gate_up[0], preferred_element_type=jnp.float32)
        upper = jnp.dot(normed, gate_up[1], preferred_element_type=jnp.float32)
        hidden = (jax.nn.silu(gate) * upper).astype(jnp.bfloat16)
        summed = jnp.dot(hidden, down_t.T, preferred_element_type=jnp.float32)
        rows = (mixed_f + summed).astype(jnp.bfloat16)
    return rows
```

```python
import jax
import jax.numpy as jnp
from jax import lax
from jax.experimental import pallas as pl
from jax.experimental.pallas import tpu as pltpu
from jax.sharding import Mesh, PartitionSpec as P

D = 4096
HD = 128
BLK = 256

beta_one = 0.9
beta_two = 0.95
adam_eps = 1e-08
adam_time = 100.0
norm_eps = 1e-05

ALL = ("xh", "y", "xl", "c", "z")
GROUP = ("xh", "y", "xl", "z")
F32 = jnp.float32
BF16 = jnp.bfloat16


def adam_new(master, moment, second, grad, clip):
    learn_rate = 2.0 / D**0.5
    g = grad.astype(F32) * clip
    m = beta_one * moment + (1.0 - beta_one) * g
    v = beta_two * second + (1.0 - beta_two) * g * g
    first_fix = 1.0 - beta_one**adam_time
    second_fix = 1.0 - beta_two**adam_time
    return master - learn_rate * (m / first_fix) / (jnp.sqrt(v / second_fix) + adam_eps)


def gate_up_body(y_ref, clip_ref, master, moment, second, grad, *outs):
    clip = clip_ref[0]
    y = y_ref[0]
    wide = master.shape[2] // 4
    new = [
        adam_new(master[s], moment[s], second[s], grad[s], clip).astype(BF16) for s in range(2)
    ]
    for me in range(4):

        @pl.when(y == me)
        def _():
            for k, out in enumerate(outs):
                lo = (me ^ k) * wide
                out[:, :wide] = new[0][:, lo : lo + wide]
                out[:, wide:] = new[1][:, lo : lo + wide]


def down_body(y_ref, clip_ref, master, moment, second, grad, *outs):
    clip = clip_ref[0]
    y = y_ref[0]
    wide = master.shape[1] // 4
    new = adam_new(master[...], moment[...], second[...], grad[...], clip).astype(BF16)
    for me in range(4):

        @pl.when(y == me)
        def _():
            for k, out in enumerate(outs):
                lo = (me ^ k) * wide
                out[:, :wide] = new[:, lo : lo + wide]
                out[:, wide:] = jnp.zeros((out.shape[0], out.shape[1] - wide), BF16)


def updated(body, y, clip, arrays, width, tile):
    stack = arrays[0].shape[:-2]
    rows, cols = arrays[0].shape[-2:]
    zeros = (0,) * len(stack)
    spec = pl.BlockSpec(stack + (tile, cols), lambda i: zeros + (i, 0))
    smem = pl.BlockSpec(memory_space=pltpu.SMEM)
    return pl.pallas_call(
        body,
        grid=(rows // tile,),
        in_specs=[smem, smem] + [spec] * 4,
        out_specs=[pl.BlockSpec((tile, width), lambda i: (i, 0))] * 4,
        out_shape=[jax.ShapeDtypeStruct((rows, width), BF16)] * 4,
        compiler_params=pltpu.CompilerParams(vmem_limit_bytes=48 << 20),
    )(y, clip, *arrays)


def first_body(xl_ref, x, *refs):
    blocks, (send, keep) = refs[:-2], refs[-2:]
    half = x.shape[0] // 2
    xl = xl_ref[0]
    for out, part in ((send, 1 - xl), (keep, xl)):
        acc = None
        for b, w in enumerate(blocks):
            lhs = x[pl.ds(pl.multiple_of(part * half, half), half), b * BLK : (b + 1) * BLK]
            dot = jnp.dot(lhs, w[...], preferred_element_type=F32)
            acc = dot if acc is None else acc + dot
        out[...] = acc.astype(out.dtype)


def first_products(xl, x, blocks):
    half, width = x.shape[0] // 2, blocks[0].shape[1]
    vmem = pl.BlockSpec(memory_space=pltpu.VMEM)
    return pl.pallas_call(
        first_body,
        in_specs=[pl.BlockSpec(memory_space=pltpu.SMEM)] + [vmem] * (1 + len(blocks)),
        out_specs=[vmem, vmem],
        out_shape=[
            jax.ShapeDtypeStruct((half, width), BF16),
            jax.ShapeDtypeStruct((half, width), F32),
        ],
        compiler_params=pltpu.CompilerParams(vmem_limit_bytes=48 << 20),
    )(xl, x, *blocks)


def hidden_body(keep, other, out):
    both = keep[...] + other[...].astype(F32)
    wide = both.shape[1] // 2
    gate, upper = both[:, :wide], both[:, wide:]
    out[:, :wide] = (gate * jax.nn.sigmoid(gate) * upper).astype(BF16)
    out[:, wide:] = jnp.zeros((out.shape[0], out.shape[1] - wide), BF16)


def second_body(xl_ref, own, other, *refs):
    blocks, out = refs[:-1], refs[-1]
    half = own.shape[0]
    xl = xl_ref[0]
    for h, part in ((own, xl), (other, 1 - xl)):
        for b, w in enumerate(blocks):
            dot = lax.dot_general(
                h[...], w[...], (((1,), (1,)), ((), ())), preferred_element_type=F32
            )
            out[pl.ds(pl.multiple_of(part * half, half), half), b * BLK : (b + 1) * BLK] = (
                dot.astype(BF16)
            )


def second_products(xl, own, other, blocks):
    vmem = pl.BlockSpec(memory_space=pltpu.VMEM)
    return pl.pallas_call(
        second_body,
        in_specs=[pl.BlockSpec(memory_space=pltpu.SMEM)] + [vmem] * (2 + len(blocks)),
        out_specs=vmem,
        out_shape=jax.ShapeDtypeStruct((2 * own.shape[0], BLK * len(blocks)), BF16),
        compiler_params=pltpu.CompilerParams(vmem_limit_bytes=48 << 20),
    )(xl, own, other, *blocks)


def attend(query, keys, values, valid, fresh_k, fresh_v, step):
    scale = query.shape[-1] ** (-0.5)
    old = jnp.einsum("rjgh,rcjh->rjgc", query, keys, preferred_element_type=F32) * scale
    old = jnp.where(valid[:, None, None, :], old, -1e30)
    new = jnp.einsum("rjgh,srjh->rjgs", query, fresh_k, preferred_element_type=F32) * scale
    allowed = jnp.arange(fresh_k.shape[0]) <= step
    new = jnp.where(allowed[None, None, None, :], new, -1e30)
    top = jnp.maximum(jnp.max(old, axis=-1, keepdims=True), jnp.max(new, axis=-1, keepdims=True))
    exp_old = jnp.exp(old - top)
    exp_new = jnp.exp(new - top)
    total = jnp.sum(exp_old, axis=-1, keepdims=True) + jnp.sum(exp_new, axis=-1, keepdims=True)
    prob_old = (exp_old / total).astype(BF16)
    prob_new = (exp_new / total).astype(BF16)
    out = jnp.einsum("rjgc,rcjh->rjgh", prob_old, values, preferred_element_type=F32)
    out = out + jnp.einsum("rjgs,srjh->rjgh", prob_new, fresh_v, preferred_element_type=F32)
    return out.reshape(out.shape[0], -1)


def pairs(axis, k):
    return [(i, i ^ k) for i in range(lax.axis_size(axis))]


def hand_out(normed, c):
    r = normed.shape[0]
    n = normed.reshape(r, 4, 2, 2, BLK)
    n = jnp.where(c == 0, n, n[:, :, :, ::-1])
    n = n.transpose(1, 2, 0, 3, 4)
    to = jnp.stack([jnp.stack([n[y ^ k] for k in range(4)], axis=2) for y in range(4)])
    to = to.reshape(1, 4, 2, 1, r, D // 2)
    to = jnp.broadcast_to(to, (2, 4, 2, 4, r, D // 2)).reshape(64, r, D // 2)
    return lax.all_to_all(to, GROUP, 0, 0).reshape(64 * r, D // 2)


def hand_back(partial, c):
    r = partial.shape[0] // 64
    got = lax.all_to_all(partial.reshape(64, r, D // 2), GROUP, 0, 0)
    got = got.reshape(2, 4, 2, 4, r, 4, 2, BLK).astype(F32)
    got = got.sum(axis=(0, 3))
    out = jnp.stack([sum(got[s, :, :, y ^ s] for s in range(4)) for y in range(4)])
    out = out.transpose(2, 0, 1, 3, 4)
    out = jnp.where(c == 0, out, out[:, :, :, ::-1])
    return out.reshape(r, D)


def shards(
    gate_up_master,
    gate_up_moment,
    gate_up_second,
    gate_up_grad,
    down_master,
    down_moment,
    down_second,
    down_grad,
    norm_gain,
    start_rows,
    queries,
    new_kv,
    kv_pool,
    page_table,
    cache_len,
):
    y, xl, c = (lax.axis_index(a) for a in ("y", "xl", "c"))
    y1, xl1 = y.astype(jnp.int32)[None], xl.astype(jnp.int32)[None]
    local_squares = jnp.sum(jnp.square(gate_up_grad.astype(F32))) + jnp.sum(
        jnp.square(down_grad.astype(F32))
    )
    squares = lax.all_to_all(jnp.broadcast_to(local_squares, (128, 128)), ALL, 0, 0)
    total = jnp.sum(squares[:, 0])
    clip = jnp.minimum(1.0, 1.0 / jnp.sqrt(total))[None]
    wide = gate_up_master.shape[2] // 4
    pad = -(-wide // 128) * 128
    gate_up = updated(
        gate_up_body,
        y1,
        clip,
        (gate_up_master, gate_up_moment, gate_up_second, gate_up_grad),
        2 * wide,
        32,
    )
    down_t = updated(
        down_body, y1, clip, (down_master, down_moment, down_second, down_grad), pad, 64
    )

    def collect(pieces):
        blocks = []
        for k, piece in enumerate(pieces):
            mine = piece if k == 0 else lax.ppermute(piece, "y", pairs("y", k))
            blocks += [mine, lax.ppermute(mine, "c", pairs("c", 1))]
        return blocks

    gate_up = collect(gate_up)
    down_t = collect(down_t)

    local_rows = start_rows.shape[0]
    key_heads = new_kv.shape[-1] // HD
    cache = kv_pool[page_table].reshape(local_rows, -1, 2, key_heads, HD)
    keys = cache[:, :, 0]
    values = cache[:, :, 1]
    valid = jnp.arange(keys.shape[1], dtype=jnp.int32)[None, :] < cache_len[:, None]
    fresh = new_kv.reshape(new_kv.shape[0], local_rows, 2, key_heads, HD)
    rows = start_rows
    attended = [
        attend(
            queries[step].reshape(local_rows, key_heads, -1, HD),
            keys,
            values,
            valid,
            fresh[:, :, 0],
            fresh[:, :, 1],
            step,
        )
        for step in range(queries.shape[0])
    ]
    for step in range(queries.shape[0]):
        mixed = (rows.astype(F32) + attended[step]).astype(BF16)
        mixed_f = mixed.astype(F32)
        normed = (
            mixed_f
            * lax.rsqrt(jnp.mean(mixed_f * mixed_f, axis=-1, keepdims=True) + norm_eps)
            * norm_gain
        ).astype(BF16)
        whole = hand_out(normed, c)
        send, keep = first_products(xl1, whole, gate_up)
        other = lax.ppermute(send, "xl", pairs("xl", 1))
        hidden = pl.pallas_call(
            hidden_body, out_shape=jax.ShapeDtypeStruct((keep.shape[0], pad), BF16)
        )(keep, other)
        hidden_other = lax.ppermute(hidden, "xl", pairs("xl", 1))
        partial = second_products(xl1, hidden, hidden_other, down_t)
        rows = (mixed_f + hand_back(partial, c)).astype(BF16)
    return rows


def solution(mesh):
    fine = Mesh(mesh.devices.reshape(2, 4, 2, 2, 4), ALL)
    fsdp, cols, rows = ("y", "xl", "c"), ("xh", "z"), ALL
    in_specs = (
        *[P(None, fsdp, cols)] * 4,
        *[P(fsdp, cols)] * 4,
        P(),
        P(rows, None),
        P(None, rows, None),
        P(None, rows, None, None),
        P(rows, None, None, None),
        P(rows, None),
        P(rows),
    )
    return jax.shard_map(
        shards, mesh=fine, in_specs=in_specs, out_specs=P(rows, None), check_vma=False
    )
```

```python
import jax
import jax.numpy as jnp
from jax import lax
from jax.experimental import pallas as pl
from jax.experimental.pallas import tpu as pltpu
from jax.sharding import Mesh, PartitionSpec as P

D = 4096
HD = 128
BLK = 256

beta_one = 0.9
beta_two = 0.95
adam_eps = 1e-08
adam_time = 100.0
norm_eps = 1e-05

ALL = ("xh", "y", "xl", "c", "z")
GROUP = ("xh", "y", "xl", "z")
F32 = jnp.float32
BF16 = jnp.bfloat16


def adam_new(master, moment, second, grad, clip):
    first_fix = 1.0 - beta_one**adam_time
    second_fix = 1.0 - beta_two**adam_time
    rate = 2.0 / D**0.5 / first_fix
    g = grad.astype(F32)
    m = (rate * beta_one) * moment + (rate * (1.0 - beta_one) * clip) * g
    v = (beta_two / second_fix) * second + ((1.0 - beta_two) / second_fix * (clip * clip)) * (g * g)
    return master - m / (v * lax.rsqrt(v) + adam_eps)


def squares_body(first, second, out, acc):
    step = pl.program_id(0)

    @pl.when(step == 0)
    def _():
        acc[...] = jnp.zeros(acc.shape, F32)

    total = acc[...]
    for block in (first[0], first[1], second[...]):
        for lo in range(0, block.shape[0], 8):
            x = block[lo : lo + 8].astype(F32)
            total = total + x * x
    acc[...] = total

    @pl.when(step == pl.num_programs(0) - 1)
    def _():
        out[...] = jnp.full(out.shape, jnp.sum(acc[...]), F32)


def sum_of_squares(first, second, tile):
    rows, cols = second.shape
    return pl.pallas_call(
        squares_body,
        grid=(rows // tile,),
        in_specs=[
            pl.BlockSpec((2, tile, cols), lambda i: (0, i, 0)),
            pl.BlockSpec((tile, cols), lambda i: (i, 0)),
        ],
        out_specs=pl.BlockSpec((128, 128), lambda i: (0, 0)),
        out_shape=jax.ShapeDtypeStruct((128, 128), F32),
        scratch_shapes=[pltpu.VMEM((8, cols), F32)],
        compiler_params=pltpu.CompilerParams(vmem_limit_bytes=48 << 20),
    )(first, second)


def gate_up_body(y_ref, clip_ref, master, moment, second, grad, *outs):
    clip = clip_ref[0]
    y = y_ref[0]
    wide = master.shape[2] // 4
    new = [
        adam_new(master[s], moment[s], second[s], grad[s], clip).astype(BF16) for s in range(2)
    ]
    for me in range(4):

        @pl.when(y == me)
        def _():
            for k, out in enumerate(outs):
                lo = (me ^ k) * wide
                out[:, :wide] = new[0][:, lo : lo + wide]
                out[:, wide:] = new[1][:, lo : lo + wide]


def down_body(y_ref, clip_ref, master, moment, second, grad, *outs):
    clip = clip_ref[0]
    y = y_ref[0]
    wide = master.shape[1] // 4
    new = adam_new(master[...], moment[...], second[...], grad[...], clip).astype(BF16)
    for me in range(4):

        @pl.when(y == me)
        def _():
            for k, out in enumerate(outs):
                lo = (me ^ k) * wide
                out[:, :wide] = new[:, lo : lo + wide]
                out[:, wide:] = jnp.zeros((out.shape[0], out.shape[1] - wide), BF16)


def updated(body, y, clip, arrays, width, tile):
    stack = arrays[0].shape[:-2]
    rows, cols = arrays[0].shape[-2:]
    zeros = (0,) * len(stack)
    spec = pl.BlockSpec(stack + (tile, cols), lambda i: zeros + (i, 0))
    smem = pl.BlockSpec(memory_space=pltpu.SMEM)
    return pl.pallas_call(
        body,
        grid=(rows // tile,),
        in_specs=[smem, smem] + [spec] * 4,
        out_specs=[pl.BlockSpec((tile, width), lambda i: (i, 0))] * 4,
        out_shape=[jax.ShapeDtypeStruct((rows, width), BF16)] * 4,
        compiler_params=pltpu.CompilerParams(vmem_limit_bytes=48 << 20),
    )(y, clip, *arrays)


def first_body(xl_ref, x, *refs):
    blocks, (send, keep) = refs[:-2], refs[-2:]
    half = x.shape[0] // 2
    xl = xl_ref[0]
    for out, part in ((send, 1 - xl), (keep, xl)):
        acc = None
        for b, w in enumerate(blocks):
            lhs = x[pl.ds(pl.multiple_of(part * half, half), half), b * BLK : (b + 1) * BLK]
            dot = jnp.dot(lhs, w[...], preferred_element_type=F32)
            acc = dot if acc is None else acc + dot
        out[...] = acc.astype(out.dtype)


def first_products(xl, x, blocks):
    half, width = x.shape[0] // 2, blocks[0].shape[1]
    vmem = pl.BlockSpec(memory_space=pltpu.VMEM)
    return pl.pallas_call(
        first_body,
        in_specs=[pl.BlockSpec(memory_space=pltpu.SMEM)] + [vmem] * (1 + len(blocks)),
        out_specs=[vmem, vmem],
        out_shape=[
            jax.ShapeDtypeStruct((half, width), BF16),
            jax.ShapeDtypeStruct((half, width), F32),
        ],
        compiler_params=pltpu.CompilerParams(vmem_limit_bytes=48 << 20),
    )(xl, x, *blocks)


def hidden_body(keep, other, out):
    both = keep[...] + other[...].astype(F32)
    wide = both.shape[1] // 2
    gate, upper = both[:, :wide], both[:, wide:]
    out[:, :wide] = (gate * jax.nn.sigmoid(gate) * upper).astype(BF16)
    out[:, wide:] = jnp.zeros((out.shape[0], out.shape[1] - wide), BF16)


def hidden_units(keep, other, width):
    vmem = pl.BlockSpec(memory_space=pltpu.VMEM)
    return pl.pallas_call(
        hidden_body,
        in_specs=[vmem, vmem],
        out_specs=vmem,
        out_shape=jax.ShapeDtypeStruct((keep.shape[0], width), BF16),
    )(keep, other)


def second_body(xl_ref, own, other, *refs):
    blocks, out = refs[:-1], refs[-1]
    half = own.shape[0]
    xl = xl_ref[0]
    for h, part in ((own, xl), (other, 1 - xl)):
        for b, w in enumerate(blocks):
            dot = lax.dot_general(
                h[...], w[...], (((1,), (1,)), ((), ())), preferred_element_type=F32
            )
            out[pl.ds(pl.multiple_of(part * half, half), half), b * BLK : (b + 1) * BLK] = (
                dot.astype(BF16)
            )


def second_products(xl, own, other, blocks):
    vmem = pl.BlockSpec(memory_space=pltpu.VMEM)
    return pl.pallas_call(
        second_body,
        in_specs=[pl.BlockSpec(memory_space=pltpu.SMEM)] + [vmem] * (2 + len(blocks)),
        out_specs=vmem,
        out_shape=jax.ShapeDtypeStruct((2 * own.shape[0], BLK * len(blocks)), BF16),
        compiler_params=pltpu.CompilerParams(vmem_limit_bytes=48 << 20),
    )(xl, own, other, *blocks)


def attention_body(pages, lens, q_ref, fresh_ref, kv_ref, out_ref, q32, fresh32, q_rows):
    steps, rows, _ = q_ref.shape
    heads = kv_ref.shape[2] // HD
    group = q_ref.shape[2] // HD // heads
    n_pages = kv_ref.shape[0] // rows
    per_head = steps * group
    count = heads * per_head
    scale = HD**-0.5
    q32[...] = q_ref[...].astype(F32)
    fresh32[...] = fresh_ref[...].astype(F32)
    ctx = n_pages * kv_ref.shape[1]
    lane = lax.broadcasted_iota(jnp.int32, (count, ctx), 1)
    step_of = lax.broadcasted_iota(jnp.int32, (count, 1), 0) % per_head // group
    for r in range(rows):
        for j in range(heads):
            for s in range(steps):
                for g in range(group):
                    at = r * count + j * per_head + s * group + g
                    lo = (j * group + g) * HD
                    q_rows[at : at + 1, :] = q32[s, r : r + 1, lo : lo + HD]

    def spread(t, r, first):
        parts = []
        for j in range(heads):
            lo = (first + j) * HD
            row = fresh32[t, r : r + 1, lo : lo + HD]
            parts.append(jnp.broadcast_to(row, (per_head, HD)))
        return jnp.concatenate(parts, axis=0)

    for r in range(rows):
        kv = [kv_ref[pages[r * n_pages + p]] for p in range(n_pages)]
        head_kv = [
            jnp.concatenate([page[:, j * HD : (j + 1) * HD] for page in kv], axis=0)
            for j in range(heads)
        ]
        q = q_rows[r * count : (r + 1) * count, :]
        q_low = q.astype(BF16)
        old = jnp.concatenate(
            [
                lax.dot_general(
                    q_low[j * per_head : (j + 1) * per_head],
                    head_kv[j],
                    (((1,), (1,)), ((), ())),
                    preferred_element_type=F32,
                )
                for j in range(heads)
            ],
            axis=0,
        )
        usable = (lane % 2 == 0) & (lane // 2 < lens[r])
        old = jnp.where(usable, old * scale, -1e30)
        top = jnp.max(old, axis=-1, keepdims=True)
        new = []
        for t in range(steps):
            score = jnp.sum(q * spread(t, r, 0), axis=-1, keepdims=True) * scale
            score = jnp.where(step_of >= t, score, -1e30)
            top = jnp.maximum(top, score)
            new.append(score)
        old = jnp.exp(old - top)
        new = [jnp.exp(n - top) for n in new]
        total = jnp.sum(old, axis=-1, keepdims=True) + sum(new)
        weights = pltpu.roll(old / total, 1, axis=1).astype(BF16)
        out = jnp.concatenate(
            [
                jnp.dot(
                    weights[j * per_head : (j + 1) * per_head],
                    head_kv[j],
                    preferred_element_type=F32,
                )
                for j in range(heads)
            ],
            axis=0,
        )
        for t in range(steps):
            out = out + (new[t] / total).astype(BF16).astype(F32) * spread(t, r, heads)
        for j in range(heads):
            for s in range(steps):
                for g in range(group):
                    lo = (j * group + g) * HD
                    at = j * per_head + s * group + g
                    out_ref[s, r : r + 1, lo : lo + HD] = out[at : at + 1, :]


def attention(page_table, cache_len, queries, new_kv, kv_pool):
    steps, rows, width = queries.shape
    kv_width = new_kv.shape[-1]
    fresh = new_kv.reshape(steps, rows, 2 * kv_width)
    pool = kv_pool.reshape(kv_pool.shape[0], -1, kv_width)
    smem, vmem = (pl.BlockSpec(memory_space=m) for m in (pltpu.SMEM, pltpu.VMEM))
    return pl.pallas_call(
        attention_body,
        in_specs=[smem, smem, vmem, vmem, vmem],
        out_specs=vmem,
        out_shape=jax.ShapeDtypeStruct((steps, rows, width), F32),
        scratch_shapes=[
            pltpu.VMEM((steps, rows, width), F32),
            pltpu.VMEM((steps, rows, 2 * kv_width), F32),
            pltpu.VMEM((steps * rows * width // HD, HD), F32),
        ],
        cost_estimate=pl.CostEstimate(
            flops=16 * steps * width * pool.shape[0] * pool.shape[1],
            transcendentals=steps * width // HD * pool.shape[0] * pool.shape[1],
            bytes_accessed=16 * pool.size,
        ),
        compiler_params=pltpu.CompilerParams(vmem_limit_bytes=48 << 20),
    )(page_table.reshape(-1), cache_len, queries, fresh, pool)


def pairs(axis, k):
    return [(i, i ^ k) for i in range(lax.axis_size(axis))]


def add_partials(c, got, total):
    for b in range(16):
        y, xl, cc = b // 4, b // 2 % 2, b % 2
        sums = []
        for j in range(2):
            acc = None
            for xh in range(2):
                for ys in range(4):
                    for z in range(4):
                        lo = ((y ^ ys) * 2 + j) * BLK
                        piece = got[xh * 32 + ys * 8 + xl * 4 + z, :, lo : lo + BLK].astype(F32)
                        acc = piece if acc is None else acc + piece
            sums.append(acc)
        total[:, b * BLK : (b + 1) * BLK] = jnp.where(c == 0, sums[cc], sums[1 - cc])


def normed_out(c, mixed, gain, normed, payload):
    mixed_f = mixed.astype(F32)
    normed[...] = (
        mixed_f * lax.rsqrt(jnp.mean(mixed_f * mixed_f, axis=-1, keepdims=True) + norm_eps) * gain
    )
    for y in range(4):
        for xl in range(2):
            for k in range(4):
                lo = ((y ^ k) * 4 + xl * 2) * BLK
                pair = normed[:, lo : lo + BLK], normed[:, lo + BLK : lo + 2 * BLK]
                for j in range(2):
                    piece = jnp.where(c == 0, pair[j], pair[1 - j]).astype(BF16)
                    at = (k * 2 + j) * BLK
                    for xh in range(2):
                        for z in range(4):
                            payload[xh * 32 + y * 8 + xl * 4 + z, :, at : at + BLK] = piece


def open_body(c_ref, rows, attended, gain, mixed, payload, normed):
    new = (rows[...].astype(F32) + attended[0]).astype(BF16)
    mixed[...] = new
    normed_out(c_ref[0], new, gain[...], normed, payload)


def next_body(c_ref, rows, got, attended, gain, mixed, payload, total, normed):
    add_partials(c_ref[0], got, total)
    done = (rows[...].astype(F32) + total[...]).astype(BF16)
    new = (done.astype(F32) + attended[1]).astype(BF16)
    mixed[...] = new
    normed_out(c_ref[0], new, gain[...], normed, payload)


def last_body(c_ref, rows, got, out, total):
    add_partials(c_ref[0], got, total)
    out[...] = (rows[...].astype(F32) + total[...]).astype(BF16)


def row_call(body, rows, scratch, payload, c, *arrays):
    shape = jax.ShapeDtypeStruct(rows.shape, BF16)
    if payload:
        shape = [shape, jax.ShapeDtypeStruct((64, rows.shape[0], D // 2), BF16)]
    vmem = pl.BlockSpec(memory_space=pltpu.VMEM)
    return pl.pallas_call(
        body,
        in_specs=[pl.BlockSpec(memory_space=pltpu.SMEM)] + [vmem] * (1 + len(arrays)),
        out_specs=[vmem, vmem] if payload else vmem,
        out_shape=shape,
        scratch_shapes=[pltpu.VMEM(rows.shape, F32)] * scratch,
        compiler_params=pltpu.CompilerParams(vmem_limit_bytes=48 << 20),
    )(c, rows, *arrays)


def shards(
    gate_up_master,
    gate_up_moment,
    gate_up_second,
    gate_up_grad,
    down_master,
    down_moment,
    down_second,
    down_grad,
    norm_gain,
    start_rows,
    queries,
    new_kv,
    kv_pool,
    page_table,
    cache_len,
):
    y, xl, c = (lax.axis_index(a).astype(jnp.int32)[None] for a in ("y", "xl", "c"))
    squares = sum_of_squares(gate_up_grad, down_grad, 64)
    squares = lax.all_to_all(squares, ALL, 0, 0)
    clip = jnp.minimum(1.0, 1.0 / jnp.sqrt(jnp.sum(squares[:, 0])))[None]
    wide = gate_up_master.shape[2] // 4
    pad = -(-wide // 128) * 128
    gate_up = updated(
        gate_up_body,
        y,
        clip,
        (gate_up_master, gate_up_moment, gate_up_second, gate_up_grad),
        2 * wide,
        32,
    )
    page_table, *gate_up = lax.optimization_barrier((page_table, *gate_up))
    attended = attention(page_table, cache_len, queries, new_kv, kv_pool)
    mixed, payload = row_call(open_body, start_rows, 1, True, c, attended, norm_gain[None])
    handed = lax.all_to_all(payload, GROUP, 0, 0)
    clip, payload = lax.optimization_barrier((clip, payload))
    down_t = updated(
        down_body, y, clip, (down_master, down_moment, down_second, down_grad), pad, 64
    )

    def over_y(pieces):
        return [p if k == 0 else lax.ppermute(p, "y", pairs("y", k)) for k, p in enumerate(pieces)]

    def over_c(pieces):
        return [q for p in pieces for q in (p, lax.ppermute(p, "c", pairs("c", 1)))]

    gate_up = over_c(over_y(gate_up))
    gate_up, down_t = lax.optimization_barrier((gate_up, down_t))
    down_t = over_y(down_t)

    for step in range(queries.shape[0]):
        whole = handed.reshape(-1, D // 2)
        send, keep = first_products(xl, whole, gate_up)
        other = lax.ppermute(send, "xl", pairs("xl", 1))
        hidden = hidden_units(keep, other, pad)
        if step == 0:
            down_t = over_c(lax.optimization_barrier((down_t, hidden))[0])
        hidden_other = lax.ppermute(hidden, "xl", pairs("xl", 1))
        partial = second_products(xl, hidden, hidden_other, down_t)
        got = lax.all_to_all(partial.reshape(64, -1, D // 2), GROUP, 0, 0)
        if step == 0:
            mixed, payload = row_call(next_body, mixed, 2, True, c, got, attended, norm_gain[None])
            handed = lax.all_to_all(payload, GROUP, 0, 0)
    return row_call(last_body, mixed, 1, False, c, got)


def solution(mesh):
    fine = Mesh(mesh.devices.reshape(2, 4, 2, 2, 4), ALL)
    fsdp, cols, rows = ("y", "xl", "c"), ("xh", "z"), ALL
    in_specs = (
        *[P(None, fsdp, cols)] * 4,
        *[P(fsdp, cols)] * 4,
        P(),
        P(rows, None),
        P(None, rows, None),
        P(None, rows, None, None),
        P(rows, None, None, None),
        P(rows, None),
        P(rows),
    )
    return jax.shard_map(
        shards, mesh=fine, in_specs=in_specs, out_specs=P(rows, None), check_vma=False
    )
```

```python
import jax
import jax.numpy as jnp
from jax import lax
from jax.experimental import pallas as pl
from jax.experimental.pallas import tpu as pltpu
from jax.sharding import Mesh, PartitionSpec as P

D = 4096
HD = 128
BLK = 256

beta_one = 0.9
beta_two = 0.95
adam_eps = 1e-08
adam_time = 100.0
norm_eps = 1e-05

ALL = ("xh", "y", "xl", "c", "z")
PLANE = ("xh", "xl", "z")
GROUP = PLANE + ("y",)
F32 = jnp.float32
BF16 = jnp.bfloat16


def adam_new(master, moment, second, grad, clip):
    first_fix = 1.0 - beta_one**adam_time
    second_fix = 1.0 - beta_two**adam_time
    rate = 2.0 / D**0.5 / first_fix
    g = grad.astype(F32)
    m = (rate * beta_one) * moment + (rate * (1.0 - beta_one) * clip) * g
    v = (beta_two / second_fix) * second + ((1.0 - beta_two) / second_fix * (clip * clip)) * (g * g)
    return master - m / (v * lax.rsqrt(v) + adam_eps)


def fetch_all(pairs_of, sems, tile):
    rows = pairs_of[0][0].shape[-2]

    def copy(i, t):
        far, near = pairs_of[i]
        lead = (slice(None),) * (len(far.shape) - 2)
        at = lead + (pl.ds(pl.multiple_of(t * tile, tile), tile),)
        return pltpu.make_async_copy(far.at[at], near.at[at], sems.at[i, t])

    for t in range(rows // tile):
        for i in range(len(pairs_of)):
            copy(i, t).start()
    return copy


def squares_body(first, second, out, near, near_second, sems):
    tile = second.shape[0] // sems.shape[1]
    copy = fetch_all([(first, near), (second, near_second)], sems, tile)
    total = jnp.zeros((8, second.shape[1]), F32)
    for t in range(sems.shape[1]):
        copy(0, t).wait()
        copy(1, t).wait()
        for lo in range(t * tile, (t + 1) * tile, 8):
            for x in (near[0, lo : lo + 8], near[1, lo : lo + 8], near_second[lo : lo + 8]):
                x = x.astype(F32)
                total = total + x * x
    out[...] = jnp.full(out.shape, jnp.sum(total), F32)


def sum_of_squares(first, second, tile):
    hbm, vmem = (pl.BlockSpec(memory_space=m) for m in (pltpu.HBM, pltpu.VMEM))
    return pl.pallas_call(
        squares_body,
        in_specs=[hbm, hbm],
        out_specs=vmem,
        out_shape=jax.ShapeDtypeStruct((128, 128), F32),
        scratch_shapes=[
            pltpu.VMEM(first.shape, first.dtype),
            pltpu.VMEM(second.shape, second.dtype),
            pltpu.SemaphoreType.DMA((2, second.shape[0] // tile)),
        ],
        compiler_params=pltpu.CompilerParams(vmem_limit_bytes=60 << 20),
    )(first, second)


def gate_up_body(y_ref, clip_ref, *refs):
    far, outs, near, sems = refs[:4], refs[4:8], refs[8:12], refs[12]
    clip = clip_ref[0]
    y = y_ref[0]
    wide = far[0].shape[2] // 4
    tile = far[0].shape[1] // sems.shape[1]
    copy = fetch_all(list(zip(far, near)), sems, tile)

    @pl.loop(0, sems.shape[1])
    def _(t):
        at = pl.ds(pl.multiple_of(t * tile, tile), tile)
        for i in range(4):
            copy(i, t).wait()
        new = [adam_new(*(a[s, at, :] for a in near), clip).astype(BF16) for s in range(2)]
        for me in range(4):

            @pl.when(y == me)
            def _():
                for k, out in enumerate(outs):
                    lo = (me ^ k) * wide
                    out[at, :wide] = new[0][:, lo : lo + wide]
                    out[at, wide:] = new[1][:, lo : lo + wide]


def updated_gate_up(y, clip, arrays, tile):
    _, rows, cols = arrays[0].shape
    smem, vmem = (pl.BlockSpec(memory_space=m) for m in (pltpu.SMEM, pltpu.VMEM))
    return pl.pallas_call(
        gate_up_body,
        in_specs=[smem, smem] + [pl.BlockSpec(memory_space=pltpu.HBM)] * 4,
        out_specs=[vmem] * 4,
        out_shape=[jax.ShapeDtypeStruct((rows, cols // 2), BF16)] * 4,
        scratch_shapes=[pltpu.VMEM(a.shape, a.dtype) for a in arrays]
        + [pltpu.SemaphoreType.DMA((4, rows // tile))],
        compiler_params=pltpu.CompilerParams(vmem_limit_bytes=54 << 20),
    )(y, clip, *arrays)


def down_body(y_ref, clip_ref, master, moment, second, grad, *outs):
    clip = clip_ref[0]
    y = y_ref[0]
    wide = master.shape[1] // 4
    new = adam_new(master[...], moment[...], second[...], grad[...], clip).astype(BF16)
    for me in range(4):

        @pl.when(y == me)
        def _():
            for k, out in enumerate(outs):
                lo = (me ^ k) * wide
                out[:, :wide] = new[:, lo : lo + wide]
                out[:, wide:] = jnp.zeros((out.shape[0], out.shape[1] - wide), BF16)


def updated_down(y, clip, arrays, width, tile):
    rows, cols = arrays[0].shape
    spec = pl.BlockSpec((tile, cols), lambda i: (i, 0))
    smem = pl.BlockSpec(memory_space=pltpu.SMEM)
    return pl.pallas_call(
        down_body,
        grid=(rows // tile,),
        in_specs=[smem, smem] + [spec] * 4,
        out_specs=[pl.BlockSpec((tile, width), lambda i: (i, 0))] * 4,
        out_shape=[jax.ShapeDtypeStruct((rows, width), BF16)] * 4,
        compiler_params=pltpu.CompilerParams(vmem_limit_bytes=14 << 20),
    )(y, clip, *arrays)


def first_body(part_ref, x, *refs):
    blocks, out = refs[:-1], refs[-1]
    half = out.shape[0]
    start = pl.multiple_of(part_ref[0] * half, half)
    acc = None
    for b, w in enumerate(blocks):
        lhs = x[pl.ds(start, half), b * BLK : (b + 1) * BLK]
        dot = jnp.dot(lhs, w[...], preferred_element_type=F32)
        acc = dot if acc is None else acc + dot
    out[...] = acc.astype(out.dtype)


def first_products(part, x, blocks, dtype):
    vmem = pl.BlockSpec(memory_space=pltpu.VMEM)
    return pl.pallas_call(
        first_body,
        in_specs=[pl.BlockSpec(memory_space=pltpu.SMEM)] + [vmem] * (1 + len(blocks)),
        out_specs=vmem,
        out_shape=jax.ShapeDtypeStruct((x.shape[0] // 2, blocks[0].shape[1]), dtype),
        compiler_params=pltpu.CompilerParams(vmem_limit_bytes=12 << 20),
    )(part, x, *blocks)


def hidden_body(keep, other, out):
    both = keep[...] + other[...].astype(F32)
    wide = both.shape[1] // 2
    gate, upper = both[:, :wide], both[:, wide:]
    out[:, :wide] = (gate * jax.nn.sigmoid(gate) * upper).astype(BF16)
    out[:, wide:] = jnp.zeros((out.shape[0], out.shape[1] - wide), BF16)


def hidden_units(keep, other, width):
    vmem = pl.BlockSpec(memory_space=pltpu.VMEM)
    return pl.pallas_call(
        hidden_body,
        in_specs=[vmem, vmem],
        out_specs=vmem,
        out_shape=jax.ShapeDtypeStruct((keep.shape[0], width), BF16),
        compiler_params=pltpu.CompilerParams(vmem_limit_bytes=4 << 20),
    )(keep, other)


def second_body(xl_ref, own, other, *refs):
    blocks, out = refs[:-1], refs[-1]
    half = own.shape[0]
    xl = xl_ref[0]
    for h, part in ((own, xl), (other, 1 - xl)):
        for b, w in enumerate(blocks):
            dot = lax.dot_general(
                h[...], w[...], (((1,), (1,)), ((), ())), preferred_element_type=F32
            )
            out[pl.ds(pl.multiple_of(part * half, half), half), b * BLK : (b + 1) * BLK] = (
                dot.astype(BF16)
            )


def second_products(xl, own, other, blocks):
    vmem = pl.BlockSpec(memory_space=pltpu.VMEM)
    return pl.pallas_call(
        second_body,
        in_specs=[pl.BlockSpec(memory_space=pltpu.SMEM)] + [vmem] * (2 + len(blocks)),
        out_specs=vmem,
        out_shape=jax.ShapeDtypeStruct((2 * own.shape[0], BLK * len(blocks)), BF16),
        compiler_params=pltpu.CompilerParams(vmem_limit_bytes=8 << 20),
    )(xl, own, other, *blocks)


def attention_body(
    pages, lens, q_ref, fresh_ref, kv_far, out_ref, kv_ref, q32, fresh32, q_rows, sems
):
    chunk = kv_far.shape[0] // sems.shape[0]
    fetches = [
        pltpu.make_async_copy(
            kv_far.at[pl.ds(i * chunk, chunk)], kv_ref.at[pl.ds(i * chunk, chunk)], sems.at[i]
        )
        for i in range(sems.shape[0])
    ]
    for fetch in fetches:
        fetch.start()
    steps, rows, _ = q_ref.shape
    heads = kv_ref.shape[2] // HD
    group = q_ref.shape[2] // HD // heads
    n_pages = kv_ref.shape[0] // rows
    per_head = steps * group
    count = heads * per_head
    scale = HD**-0.5
    q32[...] = q_ref[...].astype(F32)
    fresh32[...] = fresh_ref[...].astype(F32)
    ctx = n_pages * kv_ref.shape[1]
    lane = lax.broadcasted_iota(jnp.int32, (count, ctx), 1)
    step_of = lax.broadcasted_iota(jnp.int32, (count, 1), 0) % per_head // group
    for r in range(rows):
        for j in range(heads):
            for s in range(steps):
                for g in range(group):
                    at = r * count + j * per_head + s * group + g
                    lo = (j * group + g) * HD
                    q_rows[at : at + 1, :] = q32[s, r : r + 1, lo : lo + HD]

    def spread(t, r, first):
        parts = []
        for j in range(heads):
            lo = (first + j) * HD
            row = fresh32[t, r : r + 1, lo : lo + HD]
            parts.append(jnp.broadcast_to(row, (per_head, HD)))
        return jnp.concatenate(parts, axis=0)

    for fetch in fetches:
        fetch.wait()
    for r in range(rows):
        kv = [kv_ref[pages[r * n_pages + p]] for p in range(n_pages)]
        head_kv = [
            jnp.concatenate([page[:, j * HD : (j + 1) * HD] for page in kv], axis=0)
            for j in range(heads)
        ]
        q = q_rows[r * count : (r + 1) * count, :]
        q_low = q.astype(BF16)
        old = jnp.concatenate(
            [
                lax.dot_general(
                    q_low[j * per_head : (j + 1) * per_head],
                    head_kv[j],
                    (((1,), (1,)), ((), ())),
                    preferred_element_type=F32,
                )
                for j in range(heads)
            ],
            axis=0,
        )
        usable = (lane % 2 == 0) & (lane // 2 < lens[r])
        old = jnp.where(usable, old * scale, -1e30)
        top = jnp.max(old, axis=-1, keepdims=True)
        new = []
        for t in range(steps):
            score = jnp.sum(q * spread(t, r, 0), axis=-1, keepdims=True) * scale
            score = jnp.where(step_of >= t, score, -1e30)
            top = jnp.maximum(top, score)
            new.append(score)
        old = jnp.exp(old - top)
        new = [jnp.exp(n - top) for n in new]
        total = jnp.sum(old, axis=-1, keepdims=True) + sum(new)
        weights = pltpu.roll(old / total, 1, axis=1).astype(BF16)
        out = jnp.concatenate(
            [
                jnp.dot(
                    weights[j * per_head : (j + 1) * per_head],
                    head_kv[j],
                    preferred_element_type=F32,
                )
                for j in range(heads)
            ],
            axis=0,
        )
        for t in range(steps):
            out = out + (new[t] / total).astype(BF16).astype(F32) * spread(t, r, heads)
        for j in range(heads):
            for s in range(steps):
                for g in range(group):
                    lo = (j * group + g) * HD
                    at = j * per_head + s * group + g
                    out_ref[s, r : r + 1, lo : lo + HD] = out[at : at + 1, :]


def attention(page_table, cache_len, queries, new_kv, kv_pool):
    steps, rows, width = queries.shape
    kv_width = new_kv.shape[-1]
    fresh = new_kv.reshape(steps, rows, 2 * kv_width)
    pool = kv_pool.reshape(kv_pool.shape[0], -1, kv_width)
    smem, vmem = (pl.BlockSpec(memory_space=m) for m in (pltpu.SMEM, pltpu.VMEM))
    return pl.pallas_call(
        attention_body,
        in_specs=[smem, smem, vmem, vmem, pl.BlockSpec(memory_space=pltpu.HBM)],
        out_specs=vmem,
        out_shape=jax.ShapeDtypeStruct((steps, rows, width), F32),
        scratch_shapes=[
            pltpu.VMEM(pool.shape, pool.dtype),
            pltpu.VMEM((steps, rows, width), F32),
            pltpu.VMEM((steps, rows, 2 * kv_width), F32),
            pltpu.VMEM((steps * rows * width // HD, HD), F32),
            pltpu.SemaphoreType.DMA((8,)),
        ],
        cost_estimate=pl.CostEstimate(
            flops=16 * steps * width * pool.shape[0] * pool.shape[1],
            transcendentals=steps * width // HD * pool.shape[0] * pool.shape[1],
            bytes_accessed=16 * pool.size,
        ),
        compiler_params=pltpu.CompilerParams(vmem_limit_bytes=60 << 20),
    )(page_table.reshape(-1), cache_len, queries, fresh, pool)


def pairs(axis, k):
    return [(i, i ^ k) for i in range(lax.axis_size(axis))]


def add_partials(c, got, total):
    for b in range(16):
        y, xl, cc = b // 4, b // 2 % 2, b % 2
        sums = []
        for j in range(2):
            acc = None
            for xh in range(2):
                for ys in range(4):
                    for z in range(4):
                        lo = ((y ^ ys) * 2 + j) * BLK
                        piece = got[xh * 32 + xl * 16 + z * 4 + ys, :, lo : lo + BLK].astype(F32)
                        acc = piece if acc is None else acc + piece
            sums.append(acc)
        total[:, b * BLK : (b + 1) * BLK] = jnp.where(c == 0, sums[cc], sums[1 - cc])


def norm(mixed, gain):
    mixed = mixed.astype(F32)
    return mixed * lax.rsqrt(jnp.mean(mixed * mixed, axis=-1, keepdims=True) + norm_eps) * gain


def normed_out(c, mixed, gain, normed, payload):
    normed[...] = norm(mixed, gain)
    for y in range(4):
        for xl in range(2):
            for k in range(4):
                lo = ((y ^ k) * 4 + xl * 2) * BLK
                pair = normed[:, lo : lo + BLK], normed[:, lo + BLK : lo + 2 * BLK]
                for j in range(2):
                    piece = jnp.where(c == 0, pair[j], pair[1 - j]).astype(BF16)
                    at = (k * 2 + j) * BLK
                    for xh in range(2):
                        for z in range(4):
                            payload[xh * 32 + xl * 16 + z * 4 + y, :, at : at + BLK] = piece


def open_body(rows, attended, gain, mixed, normed):
    new = (rows[...].astype(F32) + attended[0]).astype(BF16)
    mixed[...] = new
    normed[...] = norm(new, gain[...]).astype(BF16)


def open_rows(rows, attended, gain):
    vmem = pl.BlockSpec(memory_space=pltpu.VMEM)
    return pl.pallas_call(
        open_body,
        in_specs=[vmem] * 3,
        out_specs=[vmem] * 2,
        out_shape=[jax.ShapeDtypeStruct(rows.shape, BF16)] * 2,
        compiler_params=pltpu.CompilerParams(vmem_limit_bytes=4 << 20),
    )(rows, attended, gain)


def spread_body(y_ref, c_ref, *refs):
    *rows, payload = refs
    y, c = y_ref[0], c_ref[0]
    for k, row in enumerate(rows):
        for xl in range(2):
            for b in range(8):
                lo = ((y ^ (b // 2)) * 4 + xl * 2 + (c ^ (b % 2))) * BLK
                piece = row[:, pl.ds(pl.multiple_of(lo, BLK), BLK)]
                for xh in range(2):
                    for z in range(4):
                        payload[xh * 8 + xl * 4 + z, y ^ k, :, b * BLK : (b + 1) * BLK] = piece


def spread_rows(y, c, rows):
    vmem, smem = (pl.BlockSpec(memory_space=m) for m in (pltpu.VMEM, pltpu.SMEM))
    return pl.pallas_call(
        spread_body,
        in_specs=[smem, smem] + [vmem] * 4,
        out_specs=vmem,
        out_shape=jax.ShapeDtypeStruct((16, 4, rows[0].shape[0], D // 2), BF16),
        compiler_params=pltpu.CompilerParams(vmem_limit_bytes=8 << 20),
    )(y, c, *rows)


def next_body(c_ref, rows, got, attended, gain, mixed, payload, total, normed):
    add_partials(c_ref[0], got, total)
    done = (rows[...].astype(F32) + total[...]).astype(BF16)
    new = (done.astype(F32) + attended[1]).astype(BF16)
    mixed[...] = new
    normed_out(c_ref[0], new, gain[...], normed, payload)


def last_body(c_ref, rows, got, out, total):
    add_partials(c_ref[0], got, total)
    out[...] = (rows[...].astype(F32) + total[...]).astype(BF16)


def row_call(body, rows, scratch, payload, c, *arrays):
    shape = jax.ShapeDtypeStruct(rows.shape, BF16)
    if payload:
        shape = [shape, jax.ShapeDtypeStruct((64, rows.shape[0], D // 2), BF16)]
    vmem = pl.BlockSpec(memory_space=pltpu.VMEM)
    return pl.pallas_call(
        body,
        in_specs=[pl.BlockSpec(memory_space=pltpu.SMEM)] + [vmem] * (1 + len(arrays)),
        out_specs=[vmem, vmem] if payload else vmem,
        out_shape=shape,
        scratch_shapes=[pltpu.VMEM(rows.shape, F32)] * scratch,
        compiler_params=pltpu.CompilerParams(vmem_limit_bytes=8 << 20),
    )(c, rows, *arrays)


def over_y(pieces):
    return [p if k == 0 else lax.ppermute(p, "y", pairs("y", k)) for k, p in enumerate(pieces)]


def over_c(pieces):
    return [q for p in pieces for q in (p, lax.ppermute(p, "c", pairs("c", 1)))]


def shards(
    gate_up_master,
    gate_up_moment,
    gate_up_second,
    gate_up_grad,
    down_master,
    down_moment,
    down_second,
    down_grad,
    norm_gain,
    start_rows,
    queries,
    new_kv,
    kv_pool,
    page_table,
    cache_len,
):
    y, xl, c = (lax.axis_index(a).astype(jnp.int32)[None] for a in ("y", "xl", "c"))
    squares = sum_of_squares(gate_up_grad, down_grad, 64)
    page_table, squares = lax.optimization_barrier((page_table, squares))
    squares = lax.all_to_all(squares, ALL, 0, 0)
    attended = attention(page_table, cache_len, queries, new_kv, kv_pool)
    attended, squares = lax.optimization_barrier((attended, squares))
    mixed, normed = open_rows(start_rows, attended, norm_gain[None])
    payload = spread_rows(y, c, over_y([normed] * 4))
    payload, squares = lax.optimization_barrier((payload, squares))
    handed = lax.all_to_all(payload, PLANE, 0, 0)
    clip = jnp.minimum(1.0, 1.0 / jnp.sqrt(jnp.sum(squares[:, 0])))[None]
    wide = gate_up_master.shape[2] // 4
    pad = -(-wide // 128) * 128
    gate_up = updated_gate_up(
        y, clip, (gate_up_master, gate_up_moment, gate_up_second, gate_up_grad), 32
    )
    clip, *gate_up = lax.optimization_barrier((clip, *gate_up))
    down_t = updated_down(
        y, clip, (down_master, down_moment, down_second, down_grad), pad, 64
    )

    gate_up = [lax.optimization_barrier((p, down_t))[0] for p in over_y(gate_up)]
    gate_up, down_t = over_c(gate_up), over_y(down_t)

    for step in range(queries.shape[0]):
        whole = handed.reshape(-1, D // 2)
        send = first_products(1 - xl, whole, gate_up, BF16)
        other = lax.ppermute(send, "xl", pairs("xl", 1))
        keep = first_products(xl, whole, gate_up, F32)
        hidden = hidden_units(keep, other, pad)
        hidden_other = lax.ppermute(hidden, "xl", pairs("xl", 1))
        if step == 0:
            down_t = over_c(lax.optimization_barrier((down_t, hidden_other))[0])
        partial = second_products(xl, hidden, hidden_other, down_t)
        got = lax.all_to_all(partial.reshape(64, -1, D // 2), GROUP, 0, 0)
        if step == 0:
            mixed, payload = row_call(next_body, mixed, 2, True, c, got, attended, norm_gain[None])
            handed = lax.all_to_all(payload, GROUP, 0, 0)
    return row_call(last_body, mixed, 1, False, c, got)


def solution(mesh):
    fine = Mesh(mesh.devices.reshape(2, 4, 2, 2, 4), ALL)
    fsdp, cols, rows = ("y", "xl", "c"), ("xh", "z"), ALL
    in_specs = (
        *[P(None, fsdp, cols)] * 4,
        *[P(fsdp, cols)] * 4,
        P(),
        P(rows, None),
        P(None, rows, None),
        P(None, rows, None, None),
        P(rows, None, None, None),
        P(rows, None),
        P(rows),
    )
    return jax.shard_map(
        shards, mesh=fine, in_specs=in_specs, out_specs=P(rows, None), check_vma=False
    )
```

```python
import jax
import jax.numpy as jnp
from jax import lax
from jax.experimental import pallas as pl
from jax.experimental.pallas import tpu as pltpu
from jax.sharding import Mesh, PartitionSpec as P

D = 4096
HD = 128
BLK = 256

beta_one = 0.9
beta_two = 0.95
adam_eps = 1e-08
adam_time = 100.0
norm_eps = 1e-05

ALL = ("xh", "y", "xl", "c", "z")
PLANE = ("xh", "xl", "z")
GROUP = PLANE + ("y",)
F32 = jnp.float32
BF16 = jnp.bfloat16


def adam_new(master, moment, second, grad, clip):
    first_fix = 1.0 - beta_one**adam_time
    second_fix = 1.0 - beta_two**adam_time
    rate = 2.0 / D**0.5 / first_fix
    g = grad.astype(F32)
    m = (rate * beta_one) * moment + (rate * (1.0 - beta_one) * clip) * g
    v = (beta_two / second_fix) * second + ((1.0 - beta_two) / second_fix * (clip * clip)) * (g * g)
    return master - m / (v * lax.rsqrt(v) + adam_eps)


def fetch_all(pairs_of, sems, tile):
    rows = pairs_of[0][0].shape[-2]

    def copy(i, t):
        far, near = pairs_of[i]
        lead = (slice(None),) * (len(far.shape) - 2)
        at = lead + (pl.ds(pl.multiple_of(t * tile, tile), tile),)
        return pltpu.make_async_copy(far.at[at], near.at[at], sems.at[i, t])

    for t in range(rows // tile):
        for i in range(len(pairs_of)):
            copy(i, t).start()
    return copy


def squares_body(first, second, out, near, near_second, sems):
    tile = second.shape[0] // sems.shape[1]
    copy = fetch_all([(first, near), (second, near_second)], sems, tile)
    total = jnp.zeros((8, second.shape[1]), F32)
    for t in range(sems.shape[1]):
        copy(0, t).wait()
        copy(1, t).wait()
        for lo in range(t * tile, (t + 1) * tile, 8):
            for x in (near[0, lo : lo + 8], near[1, lo : lo + 8], near_second[lo : lo + 8]):
                x = x.astype(F32)
                total = total + x * x
    out[...] = jnp.full(out.shape, jnp.sum(total), F32)


def sum_of_squares(first, second, tile):
    hbm, vmem = (pl.BlockSpec(memory_space=m) for m in (pltpu.HBM, pltpu.VMEM))
    return pl.pallas_call(
        squares_body,
        in_specs=[hbm, hbm],
        out_specs=vmem,
        out_shape=jax.ShapeDtypeStruct((128, 128), F32),
        scratch_shapes=[
            pltpu.VMEM(first.shape, first.dtype),
            pltpu.VMEM(second.shape, second.dtype),
            pltpu.SemaphoreType.DMA((2, second.shape[0] // tile)),
        ],
        compiler_params=pltpu.CompilerParams(vmem_limit_bytes=60 << 20),
    )(first, second)


def gate_up_body(y_ref, clip_ref, *refs):
    far, outs, near, sems = refs[:4], refs[4:8], refs[8:12], refs[12]
    clip = clip_ref[0]
    y = y_ref[0]
    wide = far[0].shape[2] // 4
    tile = far[0].shape[1] // sems.shape[1]
    copy = fetch_all(list(zip(far, near)), sems, tile)

    @pl.loop(0, sems.shape[1])
    def _(t):
        at = pl.ds(pl.multiple_of(t * tile, tile), tile)
        for i in range(4):
            copy(i, t).wait()
        new = [adam_new(*(a[s, at, :] for a in near), clip).astype(BF16) for s in range(2)]
        for me in range(4):

            @pl.when(y == me)
            def _():
                for k, out in enumerate(outs):
                    lo = (me ^ k) * wide
                    out[at, :wide] = new[0][:, lo : lo + wide]
                    out[at, wide:] = new[1][:, lo : lo + wide]


def updated_gate_up(y, clip, arrays, tile):
    _, rows, cols = arrays[0].shape
    smem, vmem = (pl.BlockSpec(memory_space=m) for m in (pltpu.SMEM, pltpu.VMEM))
    return pl.pallas_call(
        gate_up_body,
        in_specs=[smem, smem] + [pl.BlockSpec(memory_space=pltpu.HBM)] * 4,
        out_specs=[vmem] * 4,
        out_shape=[jax.ShapeDtypeStruct((rows, cols // 2), BF16)] * 4,
        scratch_shapes=[pltpu.VMEM(a.shape, a.dtype) for a in arrays]
        + [pltpu.SemaphoreType.DMA((4, rows // tile))],
        compiler_params=pltpu.CompilerParams(vmem_limit_bytes=54 << 20),
    )(y, clip, *arrays)


def down_body(y_ref, clip_ref, master, moment, second, grad, *outs):
    clip = clip_ref[0]
    y = y_ref[0]
    wide = master.shape[1] // 4
    new = adam_new(master[...], moment[...], second[...], grad[...], clip).astype(BF16)
    for me in range(4):

        @pl.when(y == me)
        def _():
            for k, out in enumerate(outs):
                lo = (me ^ k) * wide
                out[:, :wide] = new[:, lo : lo + wide]
                out[:, wide:] = jnp.zeros((out.shape[0], out.shape[1] - wide), BF16)


def updated_down(y, clip, arrays, width, tile):
    rows, cols = arrays[0].shape
    spec = pl.BlockSpec((tile, cols), lambda i: (i, 0))
    smem = pl.BlockSpec(memory_space=pltpu.SMEM)
    return pl.pallas_call(
        down_body,
        grid=(rows // tile,),
        in_specs=[smem, smem] + [spec] * 4,
        out_specs=[pl.BlockSpec((tile, width), lambda i: (i, 0))] * 4,
        out_shape=[jax.ShapeDtypeStruct((rows, width), BF16)] * 4,
        compiler_params=pltpu.CompilerParams(vmem_limit_bytes=14 << 20),
    )(y, clip, *arrays)


def first_body(part_ref, x, *refs):
    blocks, out = refs[:-1], refs[-1]
    half = out.shape[0]
    start = pl.multiple_of(part_ref[0] * half, half)
    acc = None
    for b, w in enumerate(blocks):
        lhs = x[pl.ds(start, half), b * BLK : (b + 1) * BLK]
        dot = jnp.dot(lhs, w[...], preferred_element_type=F32)
        acc = dot if acc is None else acc + dot
    out[...] = acc.astype(out.dtype)


def first_products(part, x, blocks, dtype):
    vmem = pl.BlockSpec(memory_space=pltpu.VMEM)
    return pl.pallas_call(
        first_body,
        in_specs=[pl.BlockSpec(memory_space=pltpu.SMEM)] + [vmem] * (1 + len(blocks)),
        out_specs=vmem,
        out_shape=jax.ShapeDtypeStruct((x.shape[0] // 2, blocks[0].shape[1]), dtype),
        compiler_params=pltpu.CompilerParams(vmem_limit_bytes=12 << 20),
    )(part, x, *blocks)


def hidden_body(keep, other, out):
    both = keep[...] + other[...].astype(F32)
    wide = both.shape[1] // 2
    gate, upper = both[:, :wide], both[:, wide:]
    out[:, :wide] = (gate * jax.nn.sigmoid(gate) * upper).astype(BF16)
    out[:, wide:] = jnp.zeros((out.shape[0], out.shape[1] - wide), BF16)


def hidden_units(keep, other, width):
    vmem = pl.BlockSpec(memory_space=pltpu.VMEM)
    return pl.pallas_call(
        hidden_body,
        in_specs=[vmem, vmem],
        out_specs=vmem,
        out_shape=jax.ShapeDtypeStruct((keep.shape[0], width), BF16),
        compiler_params=pltpu.CompilerParams(vmem_limit_bytes=4 << 20),
    )(keep, other)


def second_body(xl_ref, own, other, *refs):
    blocks, out = refs[:-1], refs[-1]
    half = own.shape[0]
    xl = xl_ref[0]
    for h, part in ((own, xl), (other, 1 - xl)):
        for b, w in enumerate(blocks):
            dot = lax.dot_general(
                h[...], w[...], (((1,), (1,)), ((), ())), preferred_element_type=F32
            )
            out[pl.ds(pl.multiple_of(part * half, half), half), b * BLK : (b + 1) * BLK] = (
                dot.astype(BF16)
            )


def second_products(xl, own, other, blocks):
    vmem = pl.BlockSpec(memory_space=pltpu.VMEM)
    return pl.pallas_call(
        second_body,
        in_specs=[pl.BlockSpec(memory_space=pltpu.SMEM)] + [vmem] * (2 + len(blocks)),
        out_specs=vmem,
        out_shape=jax.ShapeDtypeStruct((2 * own.shape[0], BLK * len(blocks)), BF16),
        compiler_params=pltpu.CompilerParams(vmem_limit_bytes=8 << 20),
    )(xl, own, other, *blocks)


def attention_body(
    pages,
    lens,
    rows_ref,
    gain_ref,
    q_ref,
    fresh_ref,
    kv_far,
    mixed_ref,
    normed_ref,
    next_ref,
    kv_ref,
    q32,
    fresh32,
    q_rows,
    opening,
    sems,
):
    n_pages = pages.shape[1]

    def fetch(r, p):
        return pltpu.make_async_copy(kv_far.at[pages[r, p]], kv_ref.at[r, p], sems.at[r, p])

    for r in range(pages.shape[0]):
        for p in range(n_pages):
            fetch(r, p).start()
    steps, rows, width = q_ref.shape
    pairs_of = kv_ref.shape[3]
    heads = pairs_of // 2
    group = width // HD // heads
    per_head = steps * group
    count = heads * per_head
    scale = HD**-0.5
    q32[...] = q_ref[...].astype(F32)
    fresh32[...] = fresh_ref[...].astype(F32)
    ctx = n_pages * kv_ref.shape[2] * pairs_of
    lane = lax.broadcasted_iota(jnp.int32, (count, ctx), 1)
    head_of = lax.broadcasted_iota(jnp.int32, (count, ctx), 0) // per_head
    own_key = lane % pairs_of == 2 * head_of
    place = jnp.where(own_key, lane // pairs_of, ctx)
    step_of = lax.broadcasted_iota(jnp.int32, (count, 1), 0) % per_head // group
    for r in range(rows):
        for j in range(heads):
            for s in range(steps):
                for g in range(group):
                    at = r * count + j * per_head + s * group + g
                    lo = (j * group + g) * HD
                    q_rows[at : at + 1, :] = q32[s, r : r + 1, lo : lo + HD]

    def spread(t, r, which):
        parts = []
        for j in range(heads):
            at = 2 * j + which
            parts.append(jnp.broadcast_to(fresh32[t, r, at : at + 1, :], (per_head, HD)))
        return jnp.concatenate(parts, axis=0)

    for r in range(rows):
        for p in range(n_pages):
            fetch(r, p).wait()
        kv = kv_ref[r].reshape(ctx, HD)
        q = q_rows[r * count : (r + 1) * count, :]
        old = lax.dot_general(
            q.astype(BF16), kv, (((1,), (1,)), ((), ())), preferred_element_type=F32
        )
        old = jnp.where(place < lens[r], old * scale, -1e30)
        top = jnp.max(old, axis=-1, keepdims=True)
        new = []
        for t in range(steps):
            score = jnp.sum(q * spread(t, r, 0), axis=-1, keepdims=True) * scale
            score = jnp.where(step_of >= t, score, -1e30)
            top = jnp.maximum(top, score)
            new.append(score)
        old = jnp.exp(old - top)
        new = [jnp.exp(n - top) for n in new]
        total = jnp.sum(old, axis=-1, keepdims=True) + sum(new)
        weights = old / total
        weights = jnp.concatenate(
            [pltpu.roll(weights[:, lo : lo + 128], 1, axis=1) for lo in range(0, ctx, 128)], axis=1
        )
        out = jnp.dot(weights.astype(BF16), kv, preferred_element_type=F32)
        for t in range(steps):
            out = out + (new[t] / total).astype(BF16).astype(F32) * spread(t, r, 1)
        for j in range(heads):
            for s in range(steps):
                for g in range(group):
                    lo = (j * group + g) * HD
                    at = j * per_head + s * group + g
                    target = opening if s == 0 else next_ref.at[s - 1]
                    target[r : r + 1, lo : lo + HD] = out[at : at + 1, :]
    mixed = (rows_ref[...].astype(F32) + opening[...]).astype(BF16)
    mixed_ref[...] = mixed
    normed_ref[...] = norm(mixed, gain_ref[...]).astype(BF16)


def attention(page_table, cache_len, start_rows, gain, queries, new_kv, kv_pool):
    steps, rows, width = queries.shape
    kv_width = new_kv.shape[-1]
    heads = kv_width // HD

    def by_head(kv):
        kv = kv.reshape(*kv.shape[:-1], heads, HD).swapaxes(-3, -2)
        return kv.reshape(*kv.shape[:-3], 2 * heads, HD)

    fresh, pool = by_head(new_kv), by_head(kv_pool)
    smem, vmem = (pl.BlockSpec(memory_space=m) for m in (pltpu.SMEM, pltpu.VMEM))
    return pl.pallas_call(
        attention_body,
        in_specs=[smem, smem] + [vmem] * 4 + [pl.BlockSpec(memory_space=pltpu.HBM)],
        out_specs=[vmem] * 3,
        out_shape=[
            jax.ShapeDtypeStruct((rows, width), BF16),
            jax.ShapeDtypeStruct((rows, width), BF16),
            jax.ShapeDtypeStruct((steps - 1, rows, width), F32),
        ],
        scratch_shapes=[
            pltpu.VMEM(page_table.shape + pool.shape[1:], pool.dtype),
            pltpu.VMEM((steps, rows, width), F32),
            pltpu.VMEM((steps, rows, 2 * heads, HD), F32),
            pltpu.VMEM((steps * rows * width // HD, HD), F32),
            pltpu.VMEM((rows, width), F32),
            pltpu.SemaphoreType.DMA(page_table.shape),
        ],
        cost_estimate=pl.CostEstimate(
            flops=16 * steps * width * pool.shape[0] * pool.shape[1] * pool.shape[2],
            transcendentals=steps * width // HD * pool.size // HD,
            bytes_accessed=16 * pool.size,
        ),
        compiler_params=pltpu.CompilerParams(vmem_limit_bytes=57 << 20),
    )(page_table, cache_len, start_rows, gain, queries, fresh, pool)


def pairs(axis, k):
    return [(i, i ^ k) for i in range(lax.axis_size(axis))]


def add_partials(c, got, total):
    for b in range(16):
        y, xl, cc = b // 4, b // 2 % 2, b % 2
        sums = []
        for j in range(2):
            acc = None
            for xh in range(2):
                for ys in range(4):
                    for z in range(4):
                        lo = ((y ^ ys) * 2 + j) * BLK
                        piece = got[xh * 32 + xl * 16 + z * 4 + ys, :, lo : lo + BLK].astype(F32)
                        acc = piece if acc is None else acc + piece
            sums.append(acc)
        total[:, b * BLK : (b + 1) * BLK] = jnp.where(c == 0, sums[cc], sums[1 - cc])


def norm(mixed, gain):
    mixed = mixed.astype(F32)
    return mixed * lax.rsqrt(jnp.mean(mixed * mixed, axis=-1, keepdims=True) + norm_eps) * gain


def normed_out(c, mixed, gain, normed, payload):
    normed[...] = norm(mixed, gain)
    for y in range(4):
        for xl in range(2):
            for k in range(4):
                lo = ((y ^ k) * 4 + xl * 2) * BLK
                pair = normed[:, lo : lo + BLK], normed[:, lo + BLK : lo + 2 * BLK]
                for j in range(2):
                    piece = jnp.where(c == 0, pair[j], pair[1 - j]).astype(BF16)
                    at = (k * 2 + j) * BLK
                    for xh in range(2):
                        for z in range(4):
                            payload[xh * 32 + xl * 16 + z * 4 + y, :, at : at + BLK] = piece


def spread_body(y_ref, c_ref, *refs):
    *rows, payload = refs
    y, c = y_ref[0], c_ref[0]
    for k, row in enumerate(rows):
        for xl in range(2):
            for b in range(8):
                lo = ((y ^ (b // 2)) * 4 + xl * 2 + (c ^ (b % 2))) * BLK
                piece = row[:, pl.ds(pl.multiple_of(lo, BLK), BLK)]
                for xh in range(2):
                    for z in range(4):
                        payload[xh * 8 + xl * 4 + z, y ^ k, :, b * BLK : (b + 1) * BLK] = piece


def spread_rows(y, c, rows):
    vmem, smem = (pl.BlockSpec(memory_space=m) for m in (pltpu.VMEM, pltpu.SMEM))
    return pl.pallas_call(
        spread_body,
        in_specs=[smem, smem] + [vmem] * 4,
        out_specs=vmem,
        out_shape=jax.ShapeDtypeStruct((16, 4, rows[0].shape[0], D // 2), BF16),
        compiler_params=pltpu.CompilerParams(vmem_limit_bytes=8 << 20),
    )(y, c, *rows)


def next_body(c_ref, rows, got, attended, gain, mixed, payload, total, normed):
    add_partials(c_ref[0], got, total)
    done = (rows[...].astype(F32) + total[...]).astype(BF16)
    new = (done.astype(F32) + attended[0]).astype(BF16)
    mixed[...] = new
    normed_out(c_ref[0], new, gain[...], normed, payload)


def last_body(c_ref, rows, got, out, total):
    add_partials(c_ref[0], got, total)
    out[...] = (rows[...].astype(F32) + total[...]).astype(BF16)


def row_call(body, rows, scratch, payload, c, *arrays):
    shape = jax.ShapeDtypeStruct(rows.shape, BF16)
    if payload:
        shape = [shape, jax.ShapeDtypeStruct((64, rows.shape[0], D // 2), BF16)]
    vmem = pl.BlockSpec(memory_space=pltpu.VMEM)
    return pl.pallas_call(
        body,
        in_specs=[pl.BlockSpec(memory_space=pltpu.SMEM)] + [vmem] * (1 + len(arrays)),
        out_specs=[vmem, vmem] if payload else vmem,
        out_shape=shape,
        scratch_shapes=[pltpu.VMEM(rows.shape, F32)] * scratch,
        compiler_params=pltpu.CompilerParams(vmem_limit_bytes=8 << 20),
    )(c, rows, *arrays)


def over_y(pieces):
    return [p if k == 0 else lax.ppermute(p, "y", pairs("y", k)) for k, p in enumerate(pieces)]


def over_c(pieces):
    return [q for p in pieces for q in (p, lax.ppermute(p, "c", pairs("c", 1)))]


def shards(
    gate_up_master,
    gate_up_moment,
    gate_up_second,
    gate_up_grad,
    down_master,
    down_moment,
    down_second,
    down_grad,
    norm_gain,
    start_rows,
    queries,
    new_kv,
    kv_pool,
    page_table,
    cache_len,
):
    y, xl, c = (lax.axis_index(a).astype(jnp.int32)[None] for a in ("y", "xl", "c"))
    squares = sum_of_squares(gate_up_grad, down_grad, 64)
    page_table, squares = lax.optimization_barrier((page_table, squares))
    squares = lax.all_to_all(squares, ALL, 0, 0)
    mixed, normed, attended = attention(
        page_table, cache_len, start_rows, norm_gain[None], queries, new_kv, kv_pool
    )
    opened = over_y([normed] * 4)
    clip = jnp.minimum(1.0, 1.0 / jnp.sqrt(jnp.sum(squares[:, 0])))[None]
    clip, normed = lax.optimization_barrier((clip, normed))
    wide = gate_up_master.shape[2] // 4
    pad = -(-wide // 128) * 128
    gate_up = updated_gate_up(
        y, clip, (gate_up_master, gate_up_moment, gate_up_second, gate_up_grad), 32
    )
    opened, gate_up = lax.optimization_barrier((opened, gate_up))
    payload = spread_rows(y, c, opened)
    handed = lax.all_to_all(payload, PLANE, 0, 0)
    clip, payload = lax.optimization_barrier((clip, payload))
    down_t = updated_down(
        y, clip, (down_master, down_moment, down_second, down_grad), pad, 64
    )

    gate_up = [lax.optimization_barrier((p, down_t))[0] for p in over_y(gate_up)]
    gate_up, down_t = over_c(gate_up), over_y(down_t)

    for step in range(queries.shape[0]):
        whole = handed.reshape(-1, D // 2)
        send = first_products(1 - xl, whole, gate_up, BF16)
        other = lax.ppermute(send, "xl", pairs("xl", 1))
        keep = first_products(xl, whole, gate_up, F32)
        hidden = hidden_units(keep, other, pad)
        hidden_other = lax.ppermute(hidden, "xl", pairs("xl", 1))
        if step == 0:
            down_t = over_c(lax.optimization_barrier((down_t, hidden_other))[0])
        partial = second_products(xl, hidden, hidden_other, down_t)
        got = lax.all_to_all(partial.reshape(64, -1, D // 2), GROUP, 0, 0)
        if step == 0:
            mixed, payload = row_call(next_body, mixed, 2, True, c, got, attended, norm_gain[None])
            handed = lax.all_to_all(payload, GROUP, 0, 0)
    return row_call(last_body, mixed, 1, False, c, got)


def solution(mesh):
    fine = Mesh(mesh.devices.reshape(2, 4, 2, 2, 4), ALL)
    fsdp, cols, rows = ("y", "xl", "c"), ("xh", "z"), ALL
    in_specs = (
        *[P(None, fsdp, cols)] * 4,
        *[P(fsdp, cols)] * 4,
        P(),
        P(rows, None),
        P(None, rows, None),
        P(None, rows, None, None),
        P(rows, None, None, None),
        P(rows, None),
        P(rows),
    )
    return jax.shard_map(
        shards, mesh=fine, in_specs=in_specs, out_specs=P(rows, None), check_vma=False
    )
```

```python
import jax
import jax.numpy as jnp
from jax import lax
from jax.experimental import pallas as pl
from jax.experimental.pallas import tpu as pltpu
from jax.sharding import Mesh, PartitionSpec as P

D = 4096
HD = 128
BLK = 256

beta_one = 0.9
beta_two = 0.95
adam_eps = 1e-08
adam_time = 100.0
norm_eps = 1e-05

ALL = ("xh", "y", "xl", "c", "z")
PLANE = ("xh", "xl", "z")
GROUP = PLANE + ("y",)
F32 = jnp.float32
BF16 = jnp.bfloat16


def adam_new(master, moment, second, grad, clip):
    first_fix = 1.0 - beta_one**adam_time
    second_fix = 1.0 - beta_two**adam_time
    rate = 2.0 / D**0.5 / first_fix
    g = grad.astype(F32)
    m = (rate * beta_one) * moment + (rate * (1.0 - beta_one) * clip) * g
    v = (beta_two / second_fix) * second + ((1.0 - beta_two) / second_fix * (clip * clip)) * (g * g)
    return master - m / (v * lax.rsqrt(v) + adam_eps)


def fetch_all(pairs_of, sems, tile):
    rows = pairs_of[0][0].shape[-2]

    def copy(i, t):
        far, near = pairs_of[i]
        lead = (slice(None),) * (len(far.shape) - 2)
        at = lead + (pl.ds(pl.multiple_of(t * tile, tile), tile),)
        return pltpu.make_async_copy(far.at[at], near.at[at], sems.at[i, t])

    for t in range(rows // tile):
        for i in range(len(pairs_of)):
            copy(i, t).start()
    return copy


def squares_body(first, second, out, near, near_second, sems):
    tile = second.shape[0] // sems.shape[1]
    copy = fetch_all([(first, near), (second, near_second)], sems, tile)
    total = jnp.zeros((8, second.shape[1]), F32)
    for t in range(sems.shape[1]):
        copy(0, t).wait()
        copy(1, t).wait()
        for lo in range(t * tile, (t + 1) * tile, 8):
            for x in (near[0, lo : lo + 8], near[1, lo : lo + 8], near_second[lo : lo + 8]):
                x = x.astype(F32)
                total = total + x * x
    out[...] = jnp.full(out.shape, jnp.sum(total), F32)


def sum_of_squares(first, second, tile):
    hbm, vmem = (pl.BlockSpec(memory_space=m) for m in (pltpu.HBM, pltpu.VMEM))
    return pl.pallas_call(
        squares_body,
        in_specs=[hbm, hbm],
        out_specs=vmem,
        out_shape=jax.ShapeDtypeStruct((128, 128), F32),
        scratch_shapes=[
            pltpu.VMEM(first.shape, first.dtype),
            pltpu.VMEM(second.shape, second.dtype),
            pltpu.SemaphoreType.DMA((2, second.shape[0] // tile)),
        ],
        compiler_params=pltpu.CompilerParams(vmem_limit_bytes=60 << 20),
    )(first, second)


def gate_up_body(y_ref, clip_ref, *refs):
    far, outs, near, sems = refs[:4], refs[4:8], refs[8:12], refs[12]
    clip = clip_ref[0]
    y = y_ref[0]
    wide = far[0].shape[2] // 4
    tile = far[0].shape[1] // sems.shape[1]
    copy = fetch_all(list(zip(far, near)), sems, tile)

    @pl.loop(0, sems.shape[1])
    def _(t):
        at = pl.ds(pl.multiple_of(t * tile, tile), tile)
        for i in range(4):
            copy(i, t).wait()
        new = [adam_new(*(a[s, at, :] for a in near), clip).astype(BF16) for s in range(2)]
        for me in range(4):

            @pl.when(y == me)
            def _():
                for k, out in enumerate(outs):
                    lo = (me ^ k) * wide
                    out[at, :wide] = new[0][:, lo : lo + wide]
                    out[at, wide:] = new[1][:, lo : lo + wide]


def updated_gate_up(y, clip, arrays, tile):
    _, rows, cols = arrays[0].shape
    smem, vmem = (pl.BlockSpec(memory_space=m) for m in (pltpu.SMEM, pltpu.VMEM))
    return pl.pallas_call(
        gate_up_body,
        in_specs=[smem, smem] + [pl.BlockSpec(memory_space=pltpu.HBM)] * 4,
        out_specs=[vmem] * 4,
        out_shape=[jax.ShapeDtypeStruct((rows, cols // 2), BF16)] * 4,
        scratch_shapes=[pltpu.VMEM(a.shape, a.dtype) for a in arrays]
        + [pltpu.SemaphoreType.DMA((4, rows // tile))],
        compiler_params=pltpu.CompilerParams(vmem_limit_bytes=54 << 20),
    )(y, clip, *arrays)


def down_body(y_ref, clip_ref, master, moment, second, grad, *outs):
    clip = clip_ref[0]
    y = y_ref[0]
    wide = master.shape[1] // 4
    new = adam_new(master[...], moment[...], second[...], grad[...], clip).astype(BF16)
    for me in range(4):

        @pl.when(y == me)
        def _():
            for k, out in enumerate(outs):
                lo = (me ^ k) * wide
                out[:, :wide] = new[:, lo : lo + wide]
                out[:, wide:] = jnp.zeros((out.shape[0], out.shape[1] - wide), BF16)


def updated_down(y, clip, arrays, width, tile):
    rows, cols = arrays[0].shape
    spec = pl.BlockSpec((tile, cols), lambda i: (i, 0))
    smem = pl.BlockSpec(memory_space=pltpu.SMEM)
    return pl.pallas_call(
        down_body,
        grid=(rows // tile,),
        in_specs=[smem, smem] + [spec] * 4,
        out_specs=[pl.BlockSpec((tile, width), lambda i: (i, 0))] * 4,
        out_shape=[jax.ShapeDtypeStruct((rows, width), BF16)] * 4,
        compiler_params=pltpu.CompilerParams(vmem_limit_bytes=14 << 20),
    )(y, clip, *arrays)


def first_body(part_ref, x, *refs):
    blocks, out = refs[:-1], refs[-1]
    half = out.shape[0]
    start = pl.multiple_of(part_ref[0] * half, half)
    acc = None
    for b, w in enumerate(blocks):
        lhs = x[pl.ds(start, half), b * BLK : (b + 1) * BLK]
        dot = jnp.dot(lhs, w[...], preferred_element_type=F32)
        acc = dot if acc is None else acc + dot
    out[...] = acc.astype(out.dtype)


def first_products(part, x, blocks, dtype):
    vmem = pl.BlockSpec(memory_space=pltpu.VMEM)
    return pl.pallas_call(
        first_body,
        in_specs=[pl.BlockSpec(memory_space=pltpu.SMEM)] + [vmem] * (1 + len(blocks)),
        out_specs=vmem,
        out_shape=jax.ShapeDtypeStruct((x.shape[0] // 2, blocks[0].shape[1]), dtype),
        compiler_params=pltpu.CompilerParams(vmem_limit_bytes=12 << 20),
    )(part, x, *blocks)


def hidden_body(keep, other, out):
    both = keep[...] + other[...].astype(F32)
    wide = both.shape[1] // 2
    gate, upper = both[:, :wide], both[:, wide:]
    out[:, :wide] = (gate * jax.nn.sigmoid(gate) * upper).astype(BF16)
    out[:, wide:] = jnp.zeros((out.shape[0], out.shape[1] - wide), BF16)


def hidden_units(keep, other, width):
    vmem = pl.BlockSpec(memory_space=pltpu.VMEM)
    return pl.pallas_call(
        hidden_body,
        in_specs=[vmem, vmem],
        out_specs=vmem,
        out_shape=jax.ShapeDtypeStruct((keep.shape[0], width), BF16),
        compiler_params=pltpu.CompilerParams(vmem_limit_bytes=4 << 20),
    )(keep, other)


def second_body(xl_ref, own, other, *refs):
    blocks, out = refs[:-1], refs[-1]
    half = own.shape[0]
    xl = xl_ref[0]
    for h, part in ((own, xl), (other, 1 - xl)):
        for b, w in enumerate(blocks):
            dot = lax.dot_general(
                h[...], w[...], (((1,), (1,)), ((), ())), preferred_element_type=F32
            )
            out[pl.ds(pl.multiple_of(part * half, half), half), b * BLK : (b + 1) * BLK] = (
                dot.astype(BF16)
            )


def second_products(xl, own, other, blocks):
    vmem = pl.BlockSpec(memory_space=pltpu.VMEM)
    return pl.pallas_call(
        second_body,
        in_specs=[pl.BlockSpec(memory_space=pltpu.SMEM)] + [vmem] * (2 + len(blocks)),
        out_specs=vmem,
        out_shape=jax.ShapeDtypeStruct((2 * own.shape[0], BLK * len(blocks)), BF16),
        compiler_params=pltpu.CompilerParams(vmem_limit_bytes=8 << 20),
    )(xl, own, other, *blocks)


def attention_body(
    pages,
    lens,
    rows_ref,
    gain_ref,
    q_ref,
    fresh_ref,
    kv_far,
    mixed_ref,
    normed_ref,
    next_ref,
    kv_ref,
    q32,
    fresh32,
    q_rows,
    opening,
    sems,
):
    n_pages = pages.shape[1]

    part = kv_far.shape[0] // sems.shape[0]
    fetches = [
        pltpu.make_async_copy(
            kv_far.at[pl.ds(i * part, part)], kv_ref.at[pl.ds(i * part, part)], sems.at[i]
        )
        for i in range(sems.shape[0])
    ]
    for fetch in fetches:
        fetch.start()
    steps, rows, width = q_ref.shape
    pairs_of = kv_ref.shape[2]
    heads = pairs_of // 2
    group = width // HD // heads
    per_head = steps * group
    count = heads * per_head
    scale = HD**-0.5
    q32[...] = q_ref[...].astype(F32)
    fresh32[...] = fresh_ref[...].astype(F32)
    ctx = n_pages * kv_ref.shape[1] * pairs_of
    lane = lax.broadcasted_iota(jnp.int32, (count, ctx), 1)
    head_of = lax.broadcasted_iota(jnp.int32, (count, ctx), 0) // per_head
    own_key = lane % pairs_of == 2 * head_of
    place = jnp.where(own_key, lane // pairs_of, ctx)
    step_of = lax.broadcasted_iota(jnp.int32, (count, 1), 0) % per_head // group
    for r in range(rows):
        for j in range(heads):
            for s in range(steps):
                for g in range(group):
                    at = r * count + j * per_head + s * group + g
                    lo = (j * group + g) * HD
                    q_rows[at : at + 1, :] = q32[s, r : r + 1, lo : lo + HD]

    def spread(t, r, which):
        parts = []
        for j in range(heads):
            at = 2 * j + which
            parts.append(jnp.broadcast_to(fresh32[t, r, at : at + 1, :], (per_head, HD)))
        return jnp.concatenate(parts, axis=0)

    for fetch in fetches:
        fetch.wait()
    for r in range(rows):
        kv = jnp.concatenate(
            [kv_ref[pages[r, p]].reshape(ctx // n_pages, HD) for p in range(n_pages)], axis=0
        )
        q = q_rows[r * count : (r + 1) * count, :]
        old = lax.dot_general(
            q.astype(BF16), kv, (((1,), (1,)), ((), ())), preferred_element_type=F32
        )
        old = jnp.where(place < lens[r], old * scale, -1e30)
        top = jnp.max(old, axis=-1, keepdims=True)
        new = []
        for t in range(steps):
            score = jnp.sum(q * spread(t, r, 0), axis=-1, keepdims=True) * scale
            score = jnp.where(step_of >= t, score, -1e30)
            top = jnp.maximum(top, score)
            new.append(score)
        old = jnp.exp(old - top)
        new = [jnp.exp(n - top) for n in new]
        total = jnp.sum(old, axis=-1, keepdims=True) + sum(new)
        weights = old / total
        weights = jnp.concatenate(
            [pltpu.roll(weights[:, lo : lo + 128], 1, axis=1) for lo in range(0, ctx, 128)], axis=1
        )
        out = jnp.dot(weights.astype(BF16), kv, preferred_element_type=F32)
        for t in range(steps):
            out = out + (new[t] / total).astype(BF16).astype(F32) * spread(t, r, 1)
        for j in range(heads):
            for s in range(steps):
                for g in range(group):
                    lo = (j * group + g) * HD
                    at = j * per_head + s * group + g
                    target = opening if s == 0 else next_ref.at[s - 1]
                    target[r : r + 1, lo : lo + HD] = out[at : at + 1, :]
    mixed = (rows_ref[...].astype(F32) + opening[...]).astype(BF16)
    mixed_ref[...] = mixed
    normed_ref[...] = norm(mixed, gain_ref[...]).astype(BF16)


def attention(page_table, cache_len, start_rows, gain, queries, new_kv, kv_pool):
    steps, rows, width = queries.shape
    kv_width = new_kv.shape[-1]
    heads = kv_width // HD

    def by_head(kv):
        kv = kv.reshape(*kv.shape[:-1], heads, HD).swapaxes(-3, -2)
        return kv.reshape(*kv.shape[:-3], 2 * heads, HD)

    fresh, pool = by_head(new_kv), by_head(kv_pool)
    smem, vmem = (pl.BlockSpec(memory_space=m) for m in (pltpu.SMEM, pltpu.VMEM))
    return pl.pallas_call(
        attention_body,
        in_specs=[smem, smem] + [vmem] * 4 + [pl.BlockSpec(memory_space=pltpu.HBM)],
        out_specs=[vmem] * 3,
        out_shape=[
            jax.ShapeDtypeStruct((rows, width), BF16),
            jax.ShapeDtypeStruct((rows, width), BF16),
            jax.ShapeDtypeStruct((steps - 1, rows, width), F32),
        ],
        scratch_shapes=[
            pltpu.VMEM(pool.shape, pool.dtype),
            pltpu.VMEM((steps, rows, width), F32),
            pltpu.VMEM((steps, rows, 2 * heads, HD), F32),
            pltpu.VMEM((steps * rows * width // HD, HD), F32),
            pltpu.VMEM((rows, width), F32),
            pltpu.SemaphoreType.DMA((16,)),
        ],
        cost_estimate=pl.CostEstimate(
            flops=16 * steps * width * pool.shape[0] * pool.shape[1] * pool.shape[2],
            transcendentals=steps * width // HD * pool.size // HD,
            bytes_accessed=16 * pool.size,
        ),
        compiler_params=pltpu.CompilerParams(vmem_limit_bytes=57 << 20),
    )(page_table, cache_len, start_rows, gain, queries, fresh, pool)


def pairs(axis, k):
    return [(i, i ^ k) for i in range(lax.axis_size(axis))]


def add_partials(c, got, total):
    for b in range(16):
        y, xl, cc = b // 4, b // 2 % 2, b % 2
        sums = []
        for j in range(2):
            acc = None
            for xh in range(2):
                for ys in range(4):
                    for z in range(4):
                        lo = ((y ^ ys) * 2 + j) * BLK
                        piece = got[xh * 32 + xl * 16 + z * 4 + ys, :, lo : lo + BLK].astype(F32)
                        acc = piece if acc is None else acc + piece
            sums.append(acc)
        total[:, b * BLK : (b + 1) * BLK] = jnp.where(c == 0, sums[cc], sums[1 - cc])


def norm(mixed, gain):
    mixed = mixed.astype(F32)
    return mixed * lax.rsqrt(jnp.mean(mixed * mixed, axis=-1, keepdims=True) + norm_eps) * gain


def normed_out(c, mixed, gain, normed, payload):
    normed[...] = norm(mixed, gain)
    for y in range(4):
        for xl in range(2):
            for k in range(4):
                lo = ((y ^ k) * 4 + xl * 2) * BLK
                pair = normed[:, lo : lo + BLK], normed[:, lo + BLK : lo + 2 * BLK]
                for j in range(2):
                    piece = jnp.where(c == 0, pair[j], pair[1 - j]).astype(BF16)
                    at = (k * 2 + j) * BLK
                    for xh in range(2):
                        for z in range(4):
                            payload[xh * 32 + xl * 16 + z * 4 + y, :, at : at + BLK] = piece


def spread_body(y_ref, c_ref, *refs):
    *rows, payload = refs
    y, c = y_ref[0], c_ref[0]
    for k, row in enumerate(rows):
        for xl in range(2):
            for b in range(8):
                lo = ((y ^ (b // 2)) * 4 + xl * 2 + (c ^ (b % 2))) * BLK
                piece = row[:, pl.ds(pl.multiple_of(lo, BLK), BLK)]
                for xh in range(2):
                    for z in range(4):
                        payload[xh * 8 + xl * 4 + z, y ^ k, :, b * BLK : (b + 1) * BLK] = piece


def spread_rows(y, c, rows):
    vmem, smem = (pl.BlockSpec(memory_space=m) for m in (pltpu.VMEM, pltpu.SMEM))
    return pl.pallas_call(
        spread_body,
        in_specs=[smem, smem] + [vmem] * 4,
        out_specs=vmem,
        out_shape=jax.ShapeDtypeStruct((16, 4, rows[0].shape[0], D // 2), BF16),
        compiler_params=pltpu.CompilerParams(vmem_limit_bytes=8 << 20),
    )(y, c, *rows)


def next_body(c_ref, rows, got, attended, gain, mixed, payload, total, normed):
    add_partials(c_ref[0], got, total)
    done = (rows[...].astype(F32) + total[...]).astype(BF16)
    new = (done.astype(F32) + attended[0]).astype(BF16)
    mixed[...] = new
    normed_out(c_ref[0], new, gain[...], normed, payload)


def last_body(c_ref, rows, got, out, total):
    add_partials(c_ref[0], got, total)
    out[...] = (rows[...].astype(F32) + total[...]).astype(BF16)


def row_call(body, rows, scratch, payload, c, *arrays):
    shape = jax.ShapeDtypeStruct(rows.shape, BF16)
    if payload:
        shape = [shape, jax.ShapeDtypeStruct((64, rows.shape[0], D // 2), BF16)]
    vmem = pl.BlockSpec(memory_space=pltpu.VMEM)
    return pl.pallas_call(
        body,
        in_specs=[pl.BlockSpec(memory_space=pltpu.SMEM)] + [vmem] * (1 + len(arrays)),
        out_specs=[vmem, vmem] if payload else vmem,
        out_shape=shape,
        scratch_shapes=[pltpu.VMEM(rows.shape, F32)] * scratch,
        compiler_params=pltpu.CompilerParams(vmem_limit_bytes=8 << 20),
    )(c, rows, *arrays)


def over_y(pieces):
    return [p if k == 0 else lax.ppermute(p, "y", pairs("y", k)) for k, p in enumerate(pieces)]


def over_c(pieces):
    return [q for p in pieces for q in (p, lax.ppermute(p, "c", pairs("c", 1)))]


def shards(
    gate_up_master,
    gate_up_moment,
    gate_up_second,
    gate_up_grad,
    down_master,
    down_moment,
    down_second,
    down_grad,
    norm_gain,
    start_rows,
    queries,
    new_kv,
    kv_pool,
    page_table,
    cache_len,
):
    y, xl, c = (lax.axis_index(a).astype(jnp.int32)[None] for a in ("y", "xl", "c"))
    squares = sum_of_squares(gate_up_grad, down_grad, 64)
    page_table, squares = lax.optimization_barrier((page_table, squares))
    squares = lax.all_to_all(squares, ALL, 0, 0)
    mixed, normed, attended = attention(
        page_table, cache_len, start_rows, norm_gain[None], queries, new_kv, kv_pool
    )
    opened = over_y([normed] * 4)
    clip = jnp.minimum(1.0, 1.0 / jnp.sqrt(jnp.sum(squares[:, 0])))[None]
    clip, normed = lax.optimization_barrier((clip, normed))
    wide = gate_up_master.shape[2] // 4
    pad = -(-wide // 128) * 128
    gate_up = updated_gate_up(
        y, clip, (gate_up_master, gate_up_moment, gate_up_second, gate_up_grad), 32
    )
    opened, gate_up = lax.optimization_barrier((opened, gate_up))
    payload = spread_rows(y, c, opened)
    handed = lax.all_to_all(payload, PLANE, 0, 0)
    clip, payload = lax.optimization_barrier((clip, payload))
    down_t = updated_down(
        y, clip, (down_master, down_moment, down_second, down_grad), pad, 64
    )

    gate_up = [lax.optimization_barrier((p, down_t))[0] for p in over_y(gate_up)]
    gate_up, down_t = over_c(gate_up), over_y(down_t)

    for step in range(queries.shape[0]):
        whole = handed.reshape(-1, D // 2)
        send = first_products(1 - xl, whole, gate_up, BF16)
        other = lax.ppermute(send, "xl", pairs("xl", 1))
        keep = first_products(xl, whole, gate_up, F32)
        hidden = hidden_units(keep, other, pad)
        hidden_other = lax.ppermute(hidden, "xl", pairs("xl", 1))
        if step == 0:
            down_t = over_c(lax.optimization_barrier((down_t, hidden_other))[0])
        partial = second_products(xl, hidden, hidden_other, down_t)
        got = lax.all_to_all(partial.reshape(64, -1, D // 2), GROUP, 0, 0)
        if step == 0:
            mixed, payload = row_call(next_body, mixed, 2, True, c, got, attended, norm_gain[None])
            handed = lax.all_to_all(payload, GROUP, 0, 0)
    return row_call(last_body, mixed, 1, False, c, got)


def solution(mesh):
    fine = Mesh(mesh.devices.reshape(2, 4, 2, 2, 4), ALL)
    fsdp, cols, rows = ("y", "xl", "c"), ("xh", "z"), ALL
    in_specs = (
        *[P(None, fsdp, cols)] * 4,
        *[P(fsdp, cols)] * 4,
        P(),
        P(rows, None),
        P(None, rows, None),
        P(None, rows, None, None),
        P(rows, None, None, None),
        P(rows, None),
        P(rows),
    )
    return jax.shard_map(
        shards, mesh=fine, in_specs=in_specs, out_specs=P(rows, None), check_vma=False
    )
```

```python
import jax
import jax.numpy as jnp
from jax import lax
from jax.experimental import pallas as pl
from jax.experimental.pallas import tpu as pltpu
from jax.sharding import Mesh, PartitionSpec as P

D = 4096
HD = 128
BLK = 256

beta_one = 0.9
beta_two = 0.95
adam_eps = 1e-08
adam_time = 100.0
norm_eps = 1e-05

ALL = ("xh", "y", "xl", "c", "z")
PLANE = ("xh", "xl", "z")
GROUP = PLANE + ("y",)
F32 = jnp.float32
BF16 = jnp.bfloat16


def adam_new(master, moment, second, grad, clip):
    first_fix = 1.0 - beta_one**adam_time
    second_fix = 1.0 - beta_two**adam_time
    rate = 2.0 / D**0.5 / first_fix
    g = grad.astype(F32)
    m = (rate * beta_one) * moment + (rate * (1.0 - beta_one) * clip) * g
    v = (beta_two / second_fix) * second + ((1.0 - beta_two) / second_fix * (clip * clip)) * (g * g)
    return master - m / (v * lax.rsqrt(v) + adam_eps)


def fetch_all(pairs_of, sems, tile):
    rows = pairs_of[0][0].shape[-2]

    def copy(i, t):
        far, near = pairs_of[i]
        lead = (slice(None),) * (len(far.shape) - 2)
        at = lead + (pl.ds(pl.multiple_of(t * tile, tile), tile),)
        return pltpu.make_async_copy(far.at[at], near.at[at], sems.at[i, t])

    for t in range(rows // tile):
        for i in range(len(pairs_of)):
            copy(i, t).start()
    return copy


def squares_body(first, second, out, near, near_second, sems):
    tile = second.shape[0] // sems.shape[1]
    copy = fetch_all([(first, near), (second, near_second)], sems, tile)
    total = jnp.zeros((8, second.shape[1]), F32)
    for t in range(sems.shape[1]):
        copy(0, t).wait()
        copy(1, t).wait()
        for lo in range(t * tile, (t + 1) * tile, 8):
            for x in (near[0, lo : lo + 8], near[1, lo : lo + 8], near_second[lo : lo + 8]):
                x = x.astype(F32)
                total = total + x * x
    out[...] = jnp.full(out.shape, jnp.sum(total), F32)


def sum_of_squares(first, second, tile):
    hbm, vmem = (pl.BlockSpec(memory_space=m) for m in (pltpu.HBM, pltpu.VMEM))
    return pl.pallas_call(
        squares_body,
        in_specs=[hbm, hbm],
        out_specs=vmem,
        out_shape=jax.ShapeDtypeStruct((128, 128), F32),
        scratch_shapes=[
            pltpu.VMEM(first.shape, first.dtype),
            pltpu.VMEM(second.shape, second.dtype),
            pltpu.SemaphoreType.DMA((2, second.shape[0] // tile)),
        ],
        compiler_params=pltpu.CompilerParams(vmem_limit_bytes=60 << 20),
    )(first, second)


def gate_up_body(y_ref, clip_ref, *refs):
    far, outs, near, sems = refs[:4], refs[4:8], refs[8:12], refs[12]
    clip = clip_ref[0]
    y = y_ref[0]
    wide = far[0].shape[2] // 4
    tile = far[0].shape[1] // sems.shape[1]
    copy = fetch_all(list(zip(far, near)), sems, tile)

    @pl.loop(0, sems.shape[1])
    def _(t):
        at = pl.ds(pl.multiple_of(t * tile, tile), tile)
        for i in range(4):
            copy(i, t).wait()
        new = [adam_new(*(a[s, at, :] for a in near), clip).astype(BF16) for s in range(2)]
        for me in range(4):

            @pl.when(y == me)
            def _():
                for k, out in enumerate(outs):
                    lo = (me ^ k) * wide
                    out[at, :wide] = new[0][:, lo : lo + wide]
                    out[at, wide:] = new[1][:, lo : lo + wide]


def updated_gate_up(y, clip, arrays, tile):
    _, rows, cols = arrays[0].shape
    smem, vmem = (pl.BlockSpec(memory_space=m) for m in (pltpu.SMEM, pltpu.VMEM))
    return pl.pallas_call(
        gate_up_body,
        in_specs=[smem, smem] + [pl.BlockSpec(memory_space=pltpu.HBM)] * 4,
        out_specs=[vmem] * 4,
        out_shape=[jax.ShapeDtypeStruct((rows, cols // 2), BF16)] * 4,
        scratch_shapes=[pltpu.VMEM(a.shape, a.dtype) for a in arrays]
        + [pltpu.SemaphoreType.DMA((4, rows // tile))],
        compiler_params=pltpu.CompilerParams(vmem_limit_bytes=54 << 20),
    )(y, clip, *arrays)


def down_body(y_ref, clip_ref, master, moment, second, grad, *outs):
    clip = clip_ref[0]
    y = y_ref[0]
    wide = master.shape[1] // 4
    new = adam_new(master[...], moment[...], second[...], grad[...], clip).astype(BF16)
    for me in range(4):

        @pl.when(y == me)
        def _():
            for k, out in enumerate(outs):
                lo = (me ^ k) * wide
                out[:, :wide] = new[:, lo : lo + wide]
                out[:, wide:] = jnp.zeros((out.shape[0], out.shape[1] - wide), BF16)


def updated_down(y, clip, arrays, width, tile):
    rows, cols = arrays[0].shape
    spec = pl.BlockSpec((tile, cols), lambda i: (i, 0))
    smem = pl.BlockSpec(memory_space=pltpu.SMEM)
    return pl.pallas_call(
        down_body,
        grid=(rows // tile,),
        in_specs=[smem, smem] + [spec] * 4,
        out_specs=[pl.BlockSpec((tile, width), lambda i: (i, 0))] * 4,
        out_shape=[jax.ShapeDtypeStruct((rows, width), BF16)] * 4,
        compiler_params=pltpu.CompilerParams(vmem_limit_bytes=14 << 20),
    )(y, clip, *arrays)


def first_body(part_ref, x, *refs):
    blocks, out = refs[:-1], refs[-1]
    half = out.shape[0]
    start = pl.multiple_of(part_ref[0] * half, half)
    acc = None
    for b, w in enumerate(blocks):
        lhs = x[pl.ds(start, half), b * BLK : (b + 1) * BLK]
        dot = jnp.dot(lhs, w[...], preferred_element_type=F32)
        acc = dot if acc is None else acc + dot
    out[...] = acc.astype(out.dtype)


def first_products(part, x, blocks, dtype):
    vmem = pl.BlockSpec(memory_space=pltpu.VMEM)
    return pl.pallas_call(
        first_body,
        in_specs=[pl.BlockSpec(memory_space=pltpu.SMEM)] + [vmem] * (1 + len(blocks)),
        out_specs=vmem,
        out_shape=jax.ShapeDtypeStruct((x.shape[0] // 2, blocks[0].shape[1]), dtype),
        compiler_params=pltpu.CompilerParams(vmem_limit_bytes=12 << 20),
    )(part, x, *blocks)


def hidden_body(keep, other, out):
    both = keep[...] + other[...].astype(F32)
    wide = both.shape[1] // 2
    gate, upper = both[:, :wide], both[:, wide:]
    out[:, :wide] = (gate * jax.nn.sigmoid(gate) * upper).astype(BF16)
    out[:, wide:] = jnp.zeros((out.shape[0], out.shape[1] - wide), BF16)


def hidden_units(keep, other, width):
    vmem = pl.BlockSpec(memory_space=pltpu.VMEM)
    return pl.pallas_call(
        hidden_body,
        in_specs=[vmem, vmem],
        out_specs=vmem,
        out_shape=jax.ShapeDtypeStruct((keep.shape[0], width), BF16),
        compiler_params=pltpu.CompilerParams(vmem_limit_bytes=4 << 20),
    )(keep, other)


def second_body(xl_ref, own, other, *refs):
    blocks, out = refs[:-1], refs[-1]
    half = own.shape[0]
    xl = xl_ref[0]
    for h, part in ((own, xl), (other, 1 - xl)):
        at = 0
        for w in blocks:
            dot = lax.dot_general(
                h[...], w[...], (((1,), (1,)), ((), ())), preferred_element_type=F32
            )
            rows = pl.ds(pl.multiple_of(part * half, half), half)
            out[rows, at : at + w.shape[0]] = dot.astype(BF16)
            at += w.shape[0]


def second_products(xl, own, other, blocks):
    vmem = pl.BlockSpec(memory_space=pltpu.VMEM)
    return pl.pallas_call(
        second_body,
        in_specs=[pl.BlockSpec(memory_space=pltpu.SMEM)] + [vmem] * (2 + len(blocks)),
        out_specs=vmem,
        out_shape=jax.ShapeDtypeStruct((2 * own.shape[0], D // 2), BF16),
        compiler_params=pltpu.CompilerParams(vmem_limit_bytes=8 << 20),
    )(xl, own, other, *blocks)


def attention_body(
    pages,
    lens,
    rows_ref,
    gain_ref,
    q_ref,
    fresh_ref,
    kv_far,
    mixed_ref,
    normed_ref,
    next_ref,
    kv_ref,
    q32,
    fresh32,
    q_rows,
    opening,
    sems,
):
    n_pages = pages.shape[1]

    part = kv_far.shape[0] // sems.shape[0]
    fetches = [
        pltpu.make_async_copy(
            kv_far.at[pl.ds(i * part, part)], kv_ref.at[pl.ds(i * part, part)], sems.at[i]
        )
        for i in range(sems.shape[0])
    ]
    for fetch in fetches:
        fetch.start()
    steps, rows, width = q_ref.shape
    pairs_of = kv_ref.shape[2]
    heads = pairs_of // 2
    group = width // HD // heads
    per_head = steps * group
    count = heads * per_head
    scale = HD**-0.5
    q32[...] = q_ref[...].astype(F32)
    fresh32[...] = fresh_ref[...].astype(F32)
    ctx = n_pages * kv_ref.shape[1] * pairs_of
    lane = lax.broadcasted_iota(jnp.int32, (count, ctx), 1)
    head_of = lax.broadcasted_iota(jnp.int32, (count, ctx), 0) // per_head
    own_key = lane % pairs_of == 2 * head_of
    place = jnp.where(own_key, lane // pairs_of, ctx)
    step_of = lax.broadcasted_iota(jnp.int32, (count, 1), 0) % per_head // group
    for r in range(rows):
        for j in range(heads):
            for s in range(steps):
                for g in range(group):
                    at = r * count + j * per_head + s * group + g
                    lo = (j * group + g) * HD
                    q_rows[at : at + 1, :] = q32[s, r : r + 1, lo : lo + HD]

    def spread(t, r, which):
        parts = []
        for j in range(heads):
            at = 2 * j + which
            parts.append(jnp.broadcast_to(fresh32[t, r, at : at + 1, :], (per_head, HD)))
        return jnp.concatenate(parts, axis=0)

    for fetch in fetches:
        fetch.wait()
    for r in range(rows):
        kv = jnp.concatenate(
            [kv_ref[pages[r, p]].reshape(ctx // n_pages, HD) for p in range(n_pages)], axis=0
        )
        q = q_rows[r * count : (r + 1) * count, :]
        old = lax.dot_general(
            q.astype(BF16), kv, (((1,), (1,)), ((), ())), preferred_element_type=F32
        )
        old = jnp.where(place < lens[r], old * scale, -1e30)
        top = jnp.max(old, axis=-1, keepdims=True)
        new = []
        for t in range(steps):
            score = jnp.sum(q * spread(t, r, 0), axis=-1, keepdims=True) * scale
            score = jnp.where(step_of >= t, score, -1e30)
            top = jnp.maximum(top, score)
            new.append(score)
        old = jnp.exp(old - top)
        new = [jnp.exp(n - top) for n in new]
        total = jnp.sum(old, axis=-1, keepdims=True) + sum(new)
        weights = old / total
        weights = jnp.concatenate(
            [pltpu.roll(weights[:, lo : lo + 128], 1, axis=1) for lo in range(0, ctx, 128)], axis=1
        )
        out = jnp.dot(weights.astype(BF16), kv, preferred_element_type=F32)
        for t in range(steps):
            out = out + (new[t] / total).astype(BF16).astype(F32) * spread(t, r, 1)
        for j in range(heads):
            for s in range(steps):
                for g in range(group):
                    lo = (j * group + g) * HD
                    at = j * per_head + s * group + g
                    target = opening if s == 0 else next_ref.at[s - 1]
                    target[r : r + 1, lo : lo + HD] = out[at : at + 1, :]
    mixed = (rows_ref[...].astype(F32) + opening[...]).astype(BF16)
    mixed_ref[...] = mixed
    normed_ref[...] = norm(mixed, gain_ref[...]).astype(BF16)


def attention(page_table, cache_len, start_rows, gain, queries, new_kv, kv_pool):
    steps, rows, width = queries.shape
    kv_width = new_kv.shape[-1]
    heads = kv_width // HD

    def by_head(kv):
        kv = kv.reshape(*kv.shape[:-1], heads, HD).swapaxes(-3, -2)
        return kv.reshape(*kv.shape[:-3], 2 * heads, HD)

    fresh, pool = by_head(new_kv), by_head(kv_pool)
    smem, vmem = (pl.BlockSpec(memory_space=m) for m in (pltpu.SMEM, pltpu.VMEM))
    return pl.pallas_call(
        attention_body,
        in_specs=[smem, smem] + [vmem] * 4 + [pl.BlockSpec(memory_space=pltpu.HBM)],
        out_specs=[vmem] * 3,
        out_shape=[
            jax.ShapeDtypeStruct((rows, width), BF16),
            jax.ShapeDtypeStruct((rows, width), BF16),
            jax.ShapeDtypeStruct((steps - 1, rows, width), F32),
        ],
        scratch_shapes=[
            pltpu.VMEM(pool.shape, pool.dtype),
            pltpu.VMEM((steps, rows, width), F32),
            pltpu.VMEM((steps, rows, 2 * heads, HD), F32),
            pltpu.VMEM((steps * rows * width // HD, HD), F32),
            pltpu.VMEM((rows, width), F32),
            pltpu.SemaphoreType.DMA((16,)),
        ],
        cost_estimate=pl.CostEstimate(
            flops=16 * steps * width * pool.shape[0] * pool.shape[1] * pool.shape[2],
            transcendentals=steps * width // HD * pool.size // HD,
            bytes_accessed=16 * pool.size,
        ),
        compiler_params=pltpu.CompilerParams(vmem_limit_bytes=57 << 20),
    )(page_table, cache_len, start_rows, gain, queries, fresh, pool)


def pairs(axis, k):
    return [(i, i ^ k) for i in range(lax.axis_size(axis))]


def add_partials(c, got, total):
    for b in range(16):
        y, xl, cc = b // 4, b // 2 % 2, b % 2
        sums = []
        for j in range(2):
            acc = None
            for xh in range(2):
                for ys in range(4):
                    for z in range(4):
                        lo = ((y ^ ys) * 2 + j) * BLK
                        piece = got[xh * 32 + xl * 16 + z * 4 + ys, :, lo : lo + BLK].astype(F32)
                        acc = piece if acc is None else acc + piece
            sums.append(acc)
        total[:, b * BLK : (b + 1) * BLK] = jnp.where(c == 0, sums[cc], sums[1 - cc])


def norm(mixed, gain):
    mixed = mixed.astype(F32)
    return mixed * lax.rsqrt(jnp.mean(mixed * mixed, axis=-1, keepdims=True) + norm_eps) * gain


def normed_out(c, mixed, gain, normed, payload):
    normed[...] = norm(mixed, gain)
    for y in range(4):
        for xl in range(2):
            for k in range(4):
                lo = ((y ^ k) * 4 + xl * 2) * BLK
                pair = normed[:, lo : lo + BLK], normed[:, lo + BLK : lo + 2 * BLK]
                for j in range(2):
                    piece = jnp.where(c == 0, pair[j], pair[1 - j]).astype(BF16)
                    at = (k * 2 + j) * BLK
                    for xh in range(2):
                        for z in range(4):
                            payload[xh * 32 + xl * 16 + z * 4 + y, :, at : at + BLK] = piece


def spread_body(y_ref, c_ref, *refs):
    *rows, payload = refs
    y, c = y_ref[0], c_ref[0]
    for k, row in enumerate(rows):
        for xl in range(2):
            for b in range(8):
                lo = ((y ^ (b // 2)) * 4 + xl * 2 + (c ^ (b % 2))) * BLK
                piece = row[:, pl.ds(pl.multiple_of(lo, BLK), BLK)]
                for xh in range(2):
                    for z in range(4):
                        payload[xh * 8 + xl * 4 + z, y ^ k, :, b * BLK : (b + 1) * BLK] = piece


def spread_rows(y, c, rows):
    vmem, smem = (pl.BlockSpec(memory_space=m) for m in (pltpu.VMEM, pltpu.SMEM))
    return pl.pallas_call(
        spread_body,
        in_specs=[smem, smem] + [vmem] * 4,
        out_specs=vmem,
        out_shape=jax.ShapeDtypeStruct((16, 4, rows[0].shape[0], D // 2), BF16),
        compiler_params=pltpu.CompilerParams(vmem_limit_bytes=8 << 20),
    )(y, c, *rows)


def next_body(c_ref, rows, got, attended, gain, mixed, payload, total, normed):
    add_partials(c_ref[0], got, total)
    done = (rows[...].astype(F32) + total[...]).astype(BF16)
    new = (done.astype(F32) + attended[0]).astype(BF16)
    mixed[...] = new
    normed_out(c_ref[0], new, gain[...], normed, payload)


def last_body(c_ref, rows, got, out, total):
    add_partials(c_ref[0], got, total)
    out[...] = (rows[...].astype(F32) + total[...]).astype(BF16)


def row_call(body, rows, scratch, payload, c, *arrays):
    shape = jax.ShapeDtypeStruct(rows.shape, BF16)
    if payload:
        shape = [shape, jax.ShapeDtypeStruct((64, rows.shape[0], D // 2), BF16)]
    vmem = pl.BlockSpec(memory_space=pltpu.VMEM)
    return pl.pallas_call(
        body,
        in_specs=[pl.BlockSpec(memory_space=pltpu.SMEM)] + [vmem] * (1 + len(arrays)),
        out_specs=[vmem, vmem] if payload else vmem,
        out_shape=shape,
        scratch_shapes=[pltpu.VMEM(rows.shape, F32)] * scratch,
        compiler_params=pltpu.CompilerParams(vmem_limit_bytes=8 << 20),
    )(c, rows, *arrays)


def over_y(pieces):
    return [p if k == 0 else lax.ppermute(p, "y", pairs("y", k)) for k, p in enumerate(pieces)]


def over_c(pieces):
    return [q for p in pieces for q in (p, lax.ppermute(p, "c", pairs("c", 1)))]


def shards(
    gate_up_master,
    gate_up_moment,
    gate_up_second,
    gate_up_grad,
    down_master,
    down_moment,
    down_second,
    down_grad,
    norm_gain,
    start_rows,
    queries,
    new_kv,
    kv_pool,
    page_table,
    cache_len,
):
    y, xl, c = (lax.axis_index(a).astype(jnp.int32)[None] for a in ("y", "xl", "c"))
    squares = sum_of_squares(gate_up_grad, down_grad, 64)
    page_table, squares = lax.optimization_barrier((page_table, squares))
    squares = lax.all_to_all(squares, ALL, 0, 0)
    mixed, normed, attended = attention(
        page_table, cache_len, start_rows, norm_gain[None], queries, new_kv, kv_pool
    )
    opened = over_y([normed] * 4)
    clip = jnp.minimum(1.0, 1.0 / jnp.sqrt(jnp.sum(squares[:, 0])))[None]
    clip, normed = lax.optimization_barrier((clip, normed))
    wide = gate_up_master.shape[2] // 4
    pad = -(-wide // 128) * 128
    gate_up = updated_gate_up(
        y, clip, (gate_up_master, gate_up_moment, gate_up_second, gate_up_grad), 32
    )
    opened, gate_up = lax.optimization_barrier((opened, gate_up))
    payload = spread_rows(y, c, opened)
    handed = lax.all_to_all(payload, PLANE, 0, 0)
    clip, payload = lax.optimization_barrier((clip, payload))
    down_t = updated_down(
        y, clip, (down_master, down_moment, down_second, down_grad), pad, 64
    )

    gate_up = [lax.optimization_barrier((p, down_t))[0] for p in over_y(gate_up)]
    gate_up, down_t = over_c(gate_up), over_y(down_t)

    for step in range(queries.shape[0]):
        whole = handed.reshape(-1, D // 2)
        send = first_products(1 - xl, whole, gate_up, BF16)
        other = lax.ppermute(send, "xl", pairs("xl", 1))
        keep = first_products(xl, whole, gate_up, F32)
        hidden = hidden_units(keep, other, pad)
        hidden_other = lax.ppermute(hidden, "xl", pairs("xl", 1))
        if step == 0:
            down_t = lax.optimization_barrier((down_t, hidden))[0]
            down_t = [
                q
                for p in down_t
                for q in (p, *(lax.ppermute(h, "c", pairs("c", 1)) for h in jnp.split(p, 2)))
            ]
        partial = second_products(xl, hidden, hidden_other, down_t)
        got = lax.all_to_all(partial.reshape(64, -1, D // 2), GROUP, 0, 0)
        if step == 0:
            mixed, payload = row_call(next_body, mixed, 2, True, c, got, attended, norm_gain[None])
            handed = lax.all_to_all(payload, GROUP, 0, 0)
    return row_call(last_body, mixed, 1, False, c, got)


def solution(mesh):
    fine = Mesh(mesh.devices.reshape(2, 4, 2, 2, 4), ALL)
    fsdp, cols, rows = ("y", "xl", "c"), ("xh", "z"), ALL
    in_specs = (
        *[P(None, fsdp, cols)] * 4,
        *[P(fsdp, cols)] * 4,
        P(),
        P(rows, None),
        P(None, rows, None),
        P(None, rows, None, None),
        P(rows, None, None, None),
        P(rows, None),
        P(rows),
    )
    return jax.shard_map(
        shards, mesh=fine, in_specs=in_specs, out_specs=P(rows, None), check_vma=False
    )
```
